768 devices in a mesh: space: 48 (over z, x_hi, core), vel: 16 (over x_lo, y).
Axes of the slice: x: 4 (x_hi: 2, x_lo: 2; x = x_hi * 2 + x_lo), y: 8, z: 12, core: 2. Of those that a mesh axis runs over, the one named last changes fastest.
Arguments:
- distribution: float32 [384, 4, 4, 2, 16384], P('space', None, None, None, 'vel'), may hold values from 0 to 15, as said below
Outputs:
- evolved: float32 [384, 4, 4, 2, 16384], P('space', None, None, None, 'vel')
The draws below stay inside these ranges and needn't reach their ends.
Inputs may be any that keep to these rules, and one draw needn't show every extreme that they name: `distribution`: every entry is non-negative.
All inputs are finite; a program needn't handle non-finite values.
Results may differ from the reference program's by a relative error of at most 0.0001.
Values sent between devices are 32-bit elements; how exact they have to be, the bound alone decides.
No kernel may reach another device: no remote copies, remote signals or barrier semaphores. Data moves between devices by JAX's collectives and lax.ppermute only.
A program may use at most 32 MiB of HBM per device.

```python
import math
import jax
import jax.numpy as jnp
from jax import lax

NV = 32
NVH = 16384
NY = 4
NZ = 4
STEPS = 3
NX = 384


speed_limit = 8.0


def draw_distribution(key, part):
    keys = jax.random.split(key, 8)
    cells = (NX, NY, NZ)
    dense_main = jax.random.uniform(keys[0], cells, jnp.float32, 0.4, 1.2)
    dense_beam = jax.random.uniform(keys[1], cells, jnp.float32, 0.1, 0.6)
    heat_main = jnp.exp(jax.random.uniform(keys[2], cells, jnp.float32, math.log(0.6), math.log(1.6)))
    heat_beam = jnp.exp(jax.random.uniform(keys[3], cells, jnp.float32, math.log(0.6), math.log(1.6)))
    drift_main = jax.random.uniform(keys[4], (3, NX, NY, NZ), jnp.float32, -0.6, 0.6)
    boost = jnp.array([1.5, 0.0, 0.0], jnp.float32)[:, None, None, None]
    drift_beam = drift_main + boost + jax.random.uniform(keys[5], (3, NX, NY, NZ), jnp.float32, -0.3, 0.3)
    factor = jnp.exp(jax.random.uniform(keys[6], (NX, NY, NZ, 2, NVH), jnp.float32, -1.15, 1.15))
    spacing = 2.0 * speed_limit / NV
    flat_index = jnp.arange(NVH, dtype=jnp.int32)
    xlevel = (flat_index // (NV * NV)).astype(jnp.float32)
    ylevel = (flat_index // NV % NV).astype(jnp.float32)
    zlevel = (flat_index % NV).astype(jnp.float32)
    direction = (2 * jnp.arange(2, dtype=jnp.int32) - 1).astype(jnp.float32)[:, None]
    xspeed = direction * ((xlevel + 0.5) * spacing)[None, :]
    yspeed = (-speed_limit + (ylevel + 0.5) * spacing)[None, :]
    zspeed = (-speed_limit + (zlevel + 0.5) * spacing)[None, :]

    def maxwellian(dense, heat, drift):

        def cell(values):
            return values[..., None, None]
        square = (xspeed - cell(drift[0])) ** 2 + (yspeed - cell(drift[1])) ** 2 + (zspeed - cell(drift[2])) ** 2
        return cell(dense) * cell(heat) ** (-1.5) * jnp.exp(-0.5 * square / cell(heat))
    return factor * (maxwellian(dense_main, heat_main, drift_main) + maxwellian(dense_beam, heat_beam, drift_beam))


def setup_inputs(seed: int = 0) -> dict:
    seeds = jax.random.split(jax.random.key(seed), 2)
    distribution = draw_distribution(jax.random.fold_in(seeds[1], 71), 0)
    return dict(distribution=distribution)


speed_limit = 8.0
courant = 1.9
diffusivity_ratio = 2.0 / 3.0
encounter_rate = 0.7
shear_power_index = 0.75


def velocity_table(offset, velocities):
    spacing = 2.0 * speed_limit / NV
    flat_index = offset + jnp.arange(velocities, dtype=jnp.int32)
    xlevel = (flat_index // (NV * NV)).astype(jnp.float32)
    ylevel = ((flat_index // NV) % NV).astype(jnp.float32)
    zlevel = (flat_index % NV).astype(jnp.float32)
    direction = (2 * jnp.arange(2, dtype=jnp.int32) - 1).astype(jnp.float32)[:, None]
    xspeed = direction * ((xlevel + 0.5) * spacing)[None, :]
    yspeed = jnp.broadcast_to((-speed_limit + (ylevel + 0.5) * spacing)[None, :], xspeed.shape)
    zspeed = jnp.broadcast_to((-speed_limit + (zlevel + 0.5) * spacing)[None, :], xspeed.shape)
    return xspeed, yspeed, zspeed


def moment_weights(xspeed, yspeed, zspeed):
    spacing = 2.0 * speed_limit / NV
    quadrature = spacing ** 3 / (2.0 * math.pi) ** 1.5
    square = xspeed * xspeed + yspeed * yspeed + zspeed * zspeed
    rows = [jnp.ones_like(xspeed), xspeed, yspeed, zspeed, xspeed * xspeed, yspeed * yspeed,
            zspeed * zspeed, xspeed * yspeed, xspeed * zspeed, yspeed * zspeed,
            xspeed * square, yspeed * square, zspeed * square]
    return quadrature * jnp.stack(rows)


def moments_of(current, weights):
    flat = current.reshape(-1, weights.shape[1] * weights.shape[2])
    table = weights.reshape(weights.shape[0], -1)
    return lax.dot_general(table, flat, (((1,), (1,)), ((), ())),
                           precision=lax.Precision.HIGHEST, preferred_element_type=jnp.float32)


def cell_fields(moments):
    matter_concentration = moments[0]
    impulse_first_axis = moments[1] / matter_concentration
    impulse_second_axis = moments[2] / matter_concentration
    impulse_third_axis = moments[3] / matter_concentration
    whole_internal_work = moments[4] + moments[5] + moments[6]
    velocity_norm_power = impulse_first_axis * impulse_first_axis + impulse_second_axis * impulse_second_axis + impulse_third_axis * impulse_third_axis
    thermal_state = (whole_internal_work / matter_concentration - velocity_norm_power) / 3.0
    along_flow = impulse_first_axis * moments[1] + impulse_second_axis * moments[2] + impulse_third_axis * moments[3]
    xheating = 0.5 * (moments[10] - 2.0 * (impulse_first_axis * moments[4] + impulse_second_axis * moments[7] + impulse_third_axis * moments[8])
                      - impulse_first_axis * whole_internal_work + velocity_norm_power * moments[1] + 2.0 * impulse_first_axis * along_flow
                      - impulse_first_axis * velocity_norm_power * matter_concentration)
    yheating = 0.5 * (moments[11] - 2.0 * (impulse_first_axis * moments[7] + impulse_second_axis * moments[5] + impulse_third_axis * moments[9])
                      - impulse_second_axis * whole_internal_work + velocity_norm_power * moments[2] + 2.0 * impulse_second_axis * along_flow
                      - impulse_second_axis * velocity_norm_power * matter_concentration)
    zheating = 0.5 * (moments[12] - 2.0 * (impulse_first_axis * moments[8] + impulse_second_axis * moments[9] + impulse_third_axis * moments[6])
                      - impulse_third_axis * whole_internal_work + velocity_norm_power * moments[3] + 2.0 * impulse_third_axis * along_flow
                      - impulse_third_axis * velocity_norm_power * matter_concentration)
    normal_stress_level = matter_concentration * thermal_state
    conduction_factor = (1.0 - diffusivity_ratio) / (5.0 * normal_stress_level * thermal_state)
    perturbation_height = matter_concentration * thermal_state ** -1.5
    surviving_share = jnp.exp(-encounter_rate * matter_concentration * thermal_state ** (1.0 - shear_power_index))
    return jnp.stack([perturbation_height, impulse_first_axis, impulse_second_axis, impulse_third_axis, 1.0 / thermal_state,
                      conduction_factor * xheating, conduction_factor * yheating, conduction_factor * zheating, surviving_share])


def collide(current, fields, xspeed, yspeed, zspeed):
    def field(which):
        return fields[which][..., None, None]
    xdrift = xspeed - field(1)
    ydrift = yspeed - field(2)
    zdrift = zspeed - field(3)
    energy = (xdrift * xdrift + ydrift * ydrift + zdrift * zdrift) * field(4)
    heat_term = xdrift * field(5) + ydrift * field(6) + zdrift * field(7)
    target = field(0) * jnp.exp(-0.5 * energy) * (1.0 + heat_term * (energy - 5.0))
    return target + (current - target) * field(8)


def sweep_shares(speed):
    courant_ratio = courant / ((NV - 1) * speed_limit / NV)
    fraction = courant_ratio * jnp.abs(speed)
    own_share = (1.0 - fraction) * (1.0 - 0.5 * fraction)
    near_share = fraction * (2.0 - fraction)
    far_share = 0.5 * fraction * (fraction - 1.0)
    forward = speed > 0.0
    nothing = jnp.zeros_like(speed)
    return (own_share, jnp.where(forward, near_share, nothing), jnp.where(forward, far_share, nothing),
            jnp.where(forward, nothing, near_share), jnp.where(forward, nothing, far_share))


def periodic_sweep(current, shares, along):
    own_share, near_back, far_back, near_front, far_front = shares
    return (own_share * current + near_back * jnp.roll(current, 1, along) + far_back * jnp.roll(current, 2, along)
            + near_front * jnp.roll(current, -1, along) + far_front * jnp.roll(current, -2, along))


def reference(distribution):
    xspeed, yspeed, zspeed = velocity_table(0, NVH)
    weights = moment_weights(xspeed, yspeed, zspeed)
    xshares = sweep_shares(xspeed)
    yshares = sweep_shares(yspeed)
    zshares = sweep_shares(zspeed)
    current = distribution
    for repeat in range(STEPS):
        moments = moments_of(current, weights)
        fields = jnp.moveaxis(cell_fields(moments).reshape(9, NX, NY, NZ), 1, 0)

        def collide_plane(pair):
            return collide(pair[0], pair[1], xspeed, yspeed, zspeed)

        relaxed = lax.map(collide_plane, (current, fields))
        padded = jnp.pad(relaxed, ((2, 2), (0, 0), (0, 0), (0, 0), (0, 0)))

        def move_plane(plane):
            window = lax.dynamic_slice_in_dim(padded, plane, 5, 0)
            own_share, near_back, far_back, near_front, far_front = xshares
            moved = (own_share * window[2] + near_back * window[1] + far_back * window[0]
                     + near_front * window[3] + far_front * window[4])
            moved = periodic_sweep(moved, yshares, 0)
            return periodic_sweep(moved, zshares, 1)

        current = lax.map(move_plane, jnp.arange(NX, dtype=jnp.int32))
    return current
```

```python
import math

import jax
import jax.numpy as jnp
from jax import lax
from jax.experimental import pallas as pl
from jax.experimental.pallas import tpu as pltpu
from jax.sharding import PartitionSpec as P


NV = 32
STEPS = 3
SPEED_LIMIT = 8.0
SPACING = 2.0 * SPEED_LIMIT / NV
LAM = 1.9 / ((NV - 1) * SPEED_LIMIT / NV)
QUAD = SPACING**3 / (2.0 * math.pi) ** 1.5
LOG2E = math.log2(math.e)
NYZ, CELLS = 16, 128
HIGHEST = lax.Precision.HIGHEST
VMEM = pl.BlockSpec(memory_space=pltpu.VMEM)
TILE = (8, 128)


def iota(axis):
    return lax.broadcasted_iota(jnp.int32, TILE, axis)


def shares(speed):
    n = LAM * jnp.abs(speed)
    return (1.0 - n) * (1.0 - 0.5 * n), n * (2.0 - n), 0.5 * n * (n - 1.0)


def yspeed(block):
    return -SPEED_LIMIT + ((4 * block + iota(1) // 32).astype(jnp.float32) + 0.5) * SPACING


def zspeed():
    return -SPEED_LIMIT + ((iota(1) % 32).astype(jnp.float32) + 0.5) * SPACING


def sweep_yz(cells, ycoef, zcoef, zforward, yforward):
    step = -1 if yforward else 1
    ya, yb, yc = ycoef
    za, zb, zc = zcoef
    mid = [
        [
            ya * cells[y][z] + yb * cells[(y + step) % 4][z] + yc * cells[(y + 2) % 4][z]
            for z in range(4)
        ]
        for y in range(4)
    ]
    return [
        [
            za * mid[y][z]
            + zb * jnp.where(zforward, mid[y][(z - 1) % 4], mid[y][(z + 1) % 4])
            + zc * mid[y][(z + 2) % 4]
            for z in range(4)
        ]
        for y in range(4)
    ]


def moments_into(g_ref, w_ref, m_ref):
    m_ref[...] = lax.dot_general(
        w_ref[...],
        g_ref[...],
        (((1,), (1,)), ((), ())),
        precision=HIGHEST,
        preferred_element_type=jnp.float32,
    )


def xabs_here():
    index = jnp.full(TILE, lax.axis_index("vel"), jnp.int32)
    return (index.astype(jnp.float32) + 0.5) * SPACING


def even_here():
    return lax.axis_index("space") % 2 == 0


def first_kernel(d_ref, g_ref, w_ref, m_ref):
    for block in range(8):
        for half in range(2):
            lanes = pl.ds(half * 1024 + block * 128, 128)
            for yz in range(NYZ):
                rows = pl.ds(yz * 16 + block * 2 + half, 8, stride=256)
                g_ref[pl.ds(yz * 8, 8), lanes] = d_ref[rows, :]
    xabs = xabs_here()
    zs = zspeed()
    row = iota(0)
    for half in range(2):
        xs = xabs if half else -xabs
        for block in range(8):
            ys = yspeed(block)
            square = xs * xs + ys * ys + zs * zs
            lanes = pl.ds(half * 1024 + block * 128, 128)
            low = [jnp.ones_like(xs), xs, ys, zs, xs * xs, ys * ys, zs * zs, xs * ys]
            high = [xs * zs, ys * zs, xs * square, ys * square, zs * square]
            for base, rows in ((0, low), (8, high)):
                tile = jnp.zeros(TILE, jnp.float32)
                for i, r in enumerate(rows):
                    tile = jnp.where(row == i, r, tile)
                w_ref[pl.ds(base, 8), lanes] = QUAD * tile
    moments_into(g_ref, w_ref, m_ref)


def cell_fields(m):
    rho = m[0]
    inv_rho = 1.0 / rho
    ux, uy, uz = m[1] * inv_rho, m[2] * inv_rho, m[3] * inv_rho
    energy = m[4] + m[5] + m[6]
    norm = ux * ux + uy * uy + uz * uz
    temp = (energy * inv_rho - norm) / 3.0
    along = ux * m[1] + uy * m[2] + uz * m[3]

    def heating(third, u, first, r0, r1, r2):
        return 0.5 * (
            third
            - 2.0 * (ux * r0 + uy * r1 + uz * r2)
            - u * energy
            + norm * first
            + 2.0 * u * along
            - u * norm * rho
        )

    xq = heating(m[10], ux, m[1], m[4], m[7], m[8])
    yq = heating(m[11], uy, m[2], m[7], m[5], m[9])
    zq = heating(m[12], uz, m[3], m[8], m[9], m[6])
    root = jnp.sqrt(temp)
    conduction = (1.0 / 3.0) / (5.0 * rho * temp * temp)
    amp = rho / (temp * root)
    retain = jnp.exp(-0.7 * rho * jnp.sqrt(root))
    k = -0.5 * LOG2E
    fold = conduction / k
    return [ux, uy, uz, k / temp, fold * xq, fold * yq, fold * zq, amp * (1.0 - retain), retain]


class Cell:
    def __init__(self, tile, xabs, zs):
        (self.ux, self.uy, uz, self.scale, self.qx, self.qy, qz, self.amp, self.retain) = [
            jnp.broadcast_to(tile[:, k : k + 1], TILE) for k in range(9)
        ]
        zd = zs - uz
        self.ez, self.hz = zd * zd * self.scale, zd * qz
        self.x = []
        for xs in (-xabs, xabs):
            xd = xs - self.ux
            self.x.append((xd * xd * self.scale, xd * self.qx))

    def yz(self, block):
        yd = yspeed(block) - self.uy
        return yd * yd * self.scale + self.ez, yd * self.qy + self.hz

    def relax(self, half, yz, current):
        e = self.x[half][0] + yz[0]
        h = self.x[half][1] + yz[1]
        return self.amp * (jnp.exp2(e) * (1.0 + h * (e + 2.5 * LOG2E))) + self.retain * current


def xmask(half, far):
    row = iota(0)
    return (row < 1 + far) if half else (row > 6 - far)


def rotated(relaxed, half):
    return pltpu.roll(relaxed, 1 if half else 7, 0), pltpu.roll(relaxed, 2 if half else 6, 0)


def placed(out, half, z):
    shift = (2 * z if half else 2 * z + 2) % 8
    return pltpu.roll(out, shift, 0) if shift else out


def outer_kernel(a_ref, g_ref, f_ref, mb_ref):
    total = a_ref[0]
    for peer in range(1, a_ref.shape[0]):
        total = total + a_ref[peer]
    fields = cell_fields([total[k : k + 1, :] for k in range(13)])
    for k, value in enumerate(fields):
        f_ref[k : k + 1, :] = value
    f_ref[...] = jnp.transpose(f_ref[...])
    xabs = xabs_here()
    _, near, far = shares(xabs)
    zero = jnp.zeros(TILE, jnp.float32)
    zs = zspeed()

    def message(half):
        n_out = jnp.where(xmask(half, 0), near, zero)
        f_out = jnp.where(xmask(half, 1), far, zero)

        def per_y(y, carry):
            packed = [zero] * 8
            for z in range(4):
                rows = pl.ds(pl.multiple_of(y * 32 + z * 8, 8), 8)
                cell = Cell(f_ref[rows, :], xabs, zs)
                for block in range(8):
                    relaxed = cell.relax(half, cell.yz(block), g_ref[rows, pl.ds(half * 1024 + block * 128, 128)])
                    r1, r2 = rotated(relaxed, half)
                    packed[block] = packed[block] + placed(n_out * r1 + f_out * r2, half, z)
            for block in range(8):
                mb_ref[pl.ds(pl.multiple_of(y * 8, 8), 8), pl.ds(block * 128, 128)] = packed[block]
            return carry

        lax.fori_loop(0, 4, per_y, 0)

    even = even_here()
    pl.when(even)(lambda: message(0))
    pl.when(jnp.logical_not(even))(lambda: message(1))


def inner_kernel(f_ref, g_ref, l_ref, ma_ref):
    xabs = xabs_here()
    own, near, far = shares(xabs)
    zero = jnp.zeros(TILE, jnp.float32)
    zs = zspeed()
    inside = [
        (jnp.where(xmask(half, 0), zero, near), jnp.where(xmask(half, 1), zero, far)) for half in range(2)
    ]

    def slab(sent):
        n_out = jnp.where(xmask(sent, 0), near, zero)
        f_out = jnp.where(xmask(sent, 1), far, zero)

        def per_y(y, carry):
            packed = [zero] * 8
            for z in range(4):
                rows = pl.ds(pl.multiple_of(y * 32 + z * 8, 8), 8)
                cell = Cell(f_ref[rows, :], xabs, zs)
                for block in range(8):
                    yz = cell.yz(block)
                    for half in range(2):
                        lanes = pl.ds(half * 1024 + block * 128, 128)
                        relaxed = cell.relax(half, yz, g_ref[rows, lanes])
                        r1, r2 = rotated(relaxed, half)
                        n_in, f_in = inside[half]
                        l_ref[rows, lanes] = own * relaxed + n_in * r1 + f_in * r2
                        if half == sent:
                            packed[block] = packed[block] + placed(n_out * r1 + f_out * r2, half, z)
            for block in range(8):
                ma_ref[pl.ds(pl.multiple_of(y * 8, 8), 8), pl.ds(block * 128, 128)] = packed[block]
            return carry

        lax.fori_loop(0, 4, per_y, 0)

    even = even_here()
    pl.when(even)(lambda: slab(1))
    pl.when(jnp.logical_not(even))(lambda: slab(0))


def sweep_kernel(l_ref, g_ref):
    zs = zspeed()
    zcoef = shares(zs)
    zforward = zs > 0.0
    for block in range(8):
        ycoef = shares(yspeed(block))
        for half in range(2):
            lanes = pl.ds(half * 1024 + block * 128, 128)
            cells = [[l_ref[pl.ds((4 * y + z) * 8, 8), lanes] for z in range(4)] for y in range(4)]
            done = sweep_yz(cells, ycoef, zcoef, zforward, block >= 4)
            for y in range(4):
                for z in range(4):
                    g_ref[pl.ds((4 * y + z) * 8, 8), lanes] = done[y][z]


def edges(g_ref, ra_ref, rb_ref, store):
    even = jnp.full(TILE, (lax.axis_index("space") + 1) % 2, jnp.int32) > 0
    zero = jnp.zeros(TILE, jnp.float32)
    zs = zspeed()
    za, zb, zc = shares(zs)
    zforward = zs > 0.0
    for block in range(8):
        ya, yb, yc = shares(yspeed(block))
        step = -1 if block >= 4 else 1
        for half in range(2):
            cells = []
            for y in range(4):
                a, b = [r[pl.ds(y * 8, 8), pl.ds(block * 128, 128)] for r in (ra_ref, rb_ref)]
                cells.append(jnp.where(even, b, a) if half else jnp.where(even, a, b))
            for y in range(4):
                mid = ya * cells[y] + yb * cells[(y + step) % 4] + yc * cells[(y + 2) % 4]
                near = jnp.where(zforward, pltpu.roll(mid, 2, 0), pltpu.roll(mid, 6, 0))
                done = za * mid + zb * near + zc * pltpu.roll(mid, 4, 0)
                for z in range(4):
                    shift = (-2 * z if half else 6 - 2 * z) % 8
                    part = pltpu.roll(done, shift, 0) if shift else done
                    rows = pl.ds((4 * y + z) * 8, 8)
                    lanes = pl.ds(half * 1024 + block * 128, 128)
                    value = g_ref[rows, lanes] + jnp.where(xmask(half, 1), part, zero)
                    store(4 * y + z, half, block, value)


def edge_kernel(g_ref, ra_ref, rb_ref, w_ref, o_ref, m_ref):
    def store(yz, half, block, value):
        o_ref[pl.ds(yz * 8, 8), pl.ds(half * 1024 + block * 128, 128)] = value

    edges(g_ref, ra_ref, rb_ref, store)
    moments_into(o_ref, w_ref, m_ref)


def last_kernel(g_ref, ra_ref, rb_ref, o_ref):
    def store(yz, half, block, value):
        o_ref[pl.ds(yz * 16 + block * 2 + half, 8, stride=256), :] = value

    edges(g_ref, ra_ref, rb_ref, store)


def call(kernel, outs, **kw):
    shapes = [pltpu.VMEM(s, jnp.float32) for s in outs]
    return lambda *args: pl.pallas_call(
        kernel, out_shape=shapes, in_specs=[VMEM] * len(args), out_specs=[VMEM] * len(outs), **kw
    )(*(pltpu.with_memory_space_constraint(a, pltpu.VMEM) for a in args))


def local(distribution):
    layers, breadth, height, halves, velocities = distribution.shape
    vel_count = lax.axis_size("vel")
    space_count = lax.axis_size("space")
    grid = (CELLS, halves * velocities)
    message = (2 * NYZ, velocities)
    stored = distribution.reshape(layers, breadth, height, halves, 8, 128).transpose(0, 1, 2, 4, 3, 5)
    stored = stored.reshape(2048, 128)
    pairs_a = [(i, i ^ 1) for i in range(space_count)]
    pairs_b = [(i, i + 1) for i in range(1, space_count - 1, 2)]
    pairs_b = pairs_b + [(j, i) for i, j in pairs_b]
    g, weights, partial_moments = call(first_kernel, [grid, (16, grid[1]), (16, CELLS)])(stored)
    for step in range(STEPS):
        everywhere = jnp.broadcast_to(partial_moments[None], (vel_count, 16, CELLS))
        gathered = lax.all_to_all(everywhere, "vel", 0, 0)
        fields, msg_b = call(outer_kernel, [(128, 128), message])(gathered, g)
        got_b = lax.ppermute(msg_b, "space", pairs_b)
        moved, msg_a = call(inner_kernel, [grid, message])(fields, g)
        got_a = lax.ppermute(msg_a, "space", pairs_a)
        (swept,) = call(sweep_kernel, [grid])(moved)
        if step + 1 < STEPS:
            g, partial_moments = call(edge_kernel, [grid, (16, CELLS)], input_output_aliases={0: 0})(
                swept, got_a, got_b, weights
            )
        else:
            (out,) = call(last_kernel, [(2048, 128)])(swept, got_a, got_b)
    out = out.reshape(layers, breadth, height, 8, halves, 128).transpose(0, 1, 2, 4, 3, 5)
    return out.reshape(distribution.shape)


def solution(mesh):
    return jax.shard_map(
        local,
        mesh=mesh,
        in_specs=(P("space", None, None, None, "vel"),),
        out_specs=P("space", None, None, None, "vel"),
        check_vma=False,
    )
```

```python
import math

import jax
import jax.numpy as jnp
from jax import lax
from jax.experimental import pallas as pl
from jax.experimental.pallas import tpu as pltpu
from jax.sharding import PartitionSpec as P


NV = 32
STEPS = 3
SPEED_LIMIT = 8.0
SPACING = 2.0 * SPEED_LIMIT / NV
LAM = 1.9 / ((NV - 1) * SPEED_LIMIT / NV)
QUAD = SPACING**3 / (2.0 * math.pi) ** 1.5
LOG2E = math.log2(math.e)
LAYERS, CELLS = 8, 128
VMEM = pl.BlockSpec(memory_space=pltpu.VMEM)
TILE = (8, 128)


def iota(axis):
    return lax.broadcasted_iota(jnp.int32, TILE, axis)


def shares(speed):
    n = LAM * jnp.abs(speed)
    return (1.0 - n) * (1.0 - 0.5 * n), n * (2.0 - n), 0.5 * n * (n - 1.0)


def yspeed(block):
    return -SPEED_LIMIT + ((4 * block + iota(1) // 32).astype(jnp.float32) + 0.5) * SPACING


def zspeed():
    return -SPEED_LIMIT + ((iota(1) % 32).astype(jnp.float32) + 0.5) * SPACING


def sweep_yz(cells, ycoef, zcoef, zforward, yforward):
    step = -1 if yforward else 1
    ya, yb, yc = ycoef
    za, zb, zc = zcoef
    mid = [
        [
            ya * cells[y][z] + yb * cells[(y + step) % 4][z] + yc * cells[(y + 2) % 4][z]
            for z in range(4)
        ]
        for y in range(4)
    ]
    return [
        [
            za * mid[y][z]
            + zb * jnp.where(zforward, mid[y][(z - 1) % 4], mid[y][(z + 1) % 4])
            + zc * mid[y][(z + 2) % 4]
            for z in range(4)
        ]
        for y in range(4)
    ]


def split(x):
    high = x.astype(jnp.bfloat16)
    rest = x - high.astype(jnp.float32)
    mid = rest.astype(jnp.bfloat16)
    return high, mid, (rest - mid.astype(jnp.float32)).astype(jnp.bfloat16)


def weighed(w_ref, x):
    n = w_ref.shape[0] // 3
    total = None
    for k, part in enumerate(split(x)):
        product = lax.dot_general(
            w_ref[0 : (3 - k) * n, :], part, (((1,), (1,)), ((), ())), preferred_element_type=jnp.float32
        )
        for j in range(3 - k):
            piece = product[j * n : (j + 1) * n, :]
            total = piece if total is None else total + piece
    return total


def xabs_here():
    index = jnp.full(TILE, lax.axis_index("vel"), jnp.int32)
    return (index.astype(jnp.float32) + 0.5) * SPACING


def even_here():
    return lax.axis_index("space") % 2 == 0


def plane(y):
    return (slice(None), pl.ds(y * 64, 64), slice(None))


def first_kernel(d_hbm, g_ref, w_ref, we_ref, m_ref, d_ref, sems):
    copies = [pltpu.make_async_copy(d_hbm.at[plane(y)], d_ref.at[plane(y)], sems.at[y]) for y in range(4)]
    for copy in copies:
        copy.start()
    xabs = xabs_here()
    zs = zspeed()
    row = iota(0)
    for half in range(2):
        xs = xabs if half else -xabs
        for block in range(8):
            ys = yspeed(block)
            square = xs * xs + ys * ys + zs * zs
            low = [jnp.ones_like(xs), xs, ys, zs, xs * xs, ys * ys, zs * zs, xs * ys]
            high = [xs * zs, ys * zs, xs * square, ys * square, zs * square]
            tiles = []
            for rows in (low, high):
                tile = jnp.zeros(TILE, jnp.float32)
                for i, r in enumerate(rows):
                    tile = jnp.where(row == i, r, tile)
                tiles.append(QUAD * tile)
            for k, part in enumerate(split(jnp.concatenate(tiles))):
                w_ref[pl.ds(k * 16, 16), pl.ds(half * 1024 + block * 128, 128)] = part
                we_ref[pl.ds(k * 32 + (1 - half) * 16, 16), pl.ds(block * 128, 128)] = part
    for y in range(4):
        copies[y].wait()
        for z in range(4):
            yz = 4 * y + z
            for block in range(8):
                for half in range(2):
                    lanes = pl.ds(half * 1024 + block * 128, 128)
                    g_ref[pl.ds(yz * 8, 8), lanes] = d_ref[:, yz * 16 + block * 2 + half, :]
    m_ref[...] = weighed(w_ref, g_ref[...])


def cell_fields(m):
    rho = m[0]
    inv_rho = 1.0 / rho
    ux, uy, uz = m[1] * inv_rho, m[2] * inv_rho, m[3] * inv_rho
    energy = m[4] + m[5] + m[6]
    norm = ux * ux + uy * uy + uz * uz
    temp = (energy * inv_rho - norm) / 3.0
    along = ux * m[1] + uy * m[2] + uz * m[3]

    def heating(third, u, first, r0, r1, r2):
        return 0.5 * (
            third
            - 2.0 * (ux * r0 + uy * r1 + uz * r2)
            - u * energy
            + norm * first
            + 2.0 * u * along
            - u * norm * rho
        )

    xq = heating(m[10], ux, m[1], m[4], m[7], m[8])
    yq = heating(m[11], uy, m[2], m[7], m[5], m[9])
    zq = heating(m[12], uz, m[3], m[8], m[9], m[6])
    root = jnp.sqrt(temp)
    conduction = (1.0 / 3.0) / (5.0 * rho * temp * temp)
    amp = rho / (temp * root)
    retain = jnp.exp(-0.7 * rho * jnp.sqrt(root))
    k = -0.5 * LOG2E
    fold = conduction / k
    return [ux, uy, uz, k / temp, fold * xq, fold * yq, fold * zq, amp * (1.0 - retain), retain]


class Cell:
    def __init__(self, tile, xabs, zs):
        (self.ux, self.uy, uz, self.scale, self.qx, self.qy, qz, self.amp, self.retain) = [
            jnp.broadcast_to(tile[:, k : k + 1], TILE) for k in range(9)
        ]
        zd = zs - uz
        self.ez, self.hz = zd * zd * self.scale, zd * qz
        self.x = []
        for xs in (-xabs, xabs):
            xd = xs - self.ux
            self.x.append((xd * xd * self.scale, xd * self.qx))

    def yz(self, block):
        yd = yspeed(block) - self.uy
        return yd * yd * self.scale + self.ez, yd * self.qy + self.hz

    def relax(self, half, yz, current):
        e = self.x[half][0] + yz[0]
        h = self.x[half][1] + yz[1]
        return self.amp * (jnp.exp2(e) * (1.0 + h * (e + 2.5 * LOG2E))) + self.retain * current


def xmask(half, far):
    row = iota(0)
    return (row < 1 + far) if half else (row > 6 - far)


def rotated(relaxed, half):
    return pltpu.roll(relaxed, 1 if half else 7, 0), pltpu.roll(relaxed, 2 if half else 6, 0)


def placed(out, half, z):
    shift = (2 * z if half else 2 * z + 2) % 8
    return pltpu.roll(out, shift, 0) if shift else out


def outer_kernel(a_ref, g_ref, f_ref, mb_ref):
    total = a_ref[0]
    for peer in range(1, a_ref.shape[0]):
        total = total + a_ref[peer]
    fields = cell_fields([total[k : k + 1, :] for k in range(13)])
    for k, value in enumerate(fields):
        f_ref[k : k + 1, :] = value
    f_ref[...] = jnp.transpose(f_ref[...])
    xabs = xabs_here()
    _, near, far = shares(xabs)
    zero = jnp.zeros(TILE, jnp.float32)
    zs = zspeed()

    def message(half):
        n_out = jnp.where(xmask(half, 0), near, zero)
        f_out = jnp.where(xmask(half, 1), far, zero)

        def per_y(y, carry):
            packed = [zero] * 8
            for z in range(4):
                rows = pl.ds(pl.multiple_of(y * 32 + z * 8, 8), 8)
                cell = Cell(f_ref[rows, :], xabs, zs)
                for block in range(8):
                    relaxed = cell.relax(half, cell.yz(block), g_ref[rows, pl.ds(half * 1024 + block * 128, 128)])
                    r1, r2 = rotated(relaxed, half)
                    packed[block] = packed[block] + placed(n_out * r1 + f_out * r2, half, z)
            for block in range(8):
                mb_ref[pl.ds(pl.multiple_of(y * 8, 8), 8), pl.ds(block * 128, 128)] = packed[block]
            return carry

        lax.fori_loop(0, 4, per_y, 0)

    even = even_here()
    pl.when(even)(lambda: message(0))
    pl.when(jnp.logical_not(even))(lambda: message(1))


def inner_kernel(f_ref, g_ref, l_ref, ma_ref):
    xabs = xabs_here()
    own, near, far = shares(xabs)
    zero = jnp.zeros(TILE, jnp.float32)
    zs = zspeed()
    inside = [
        (jnp.where(xmask(half, 0), zero, near), jnp.where(xmask(half, 1), zero, far)) for half in range(2)
    ]

    def slab(sent):
        n_out = jnp.where(xmask(sent, 0), near, zero)
        f_out = jnp.where(xmask(sent, 1), far, zero)

        def per_y(y, carry):
            packed = [zero] * 8
            for z in range(4):
                rows = pl.ds(pl.multiple_of(y * 32 + z * 8, 8), 8)
                cell = Cell(f_ref[rows, :], xabs, zs)
                for block in range(8):
                    yz = cell.yz(block)
                    for half in range(2):
                        lanes = pl.ds(half * 1024 + block * 128, 128)
                        relaxed = cell.relax(half, yz, g_ref[rows, lanes])
                        r1, r2 = rotated(relaxed, half)
                        n_in, f_in = inside[half]
                        l_ref[rows, lanes] = own * relaxed + n_in * r1 + f_in * r2
                        if half == sent:
                            packed[block] = packed[block] + placed(n_out * r1 + f_out * r2, half, z)
            for block in range(8):
                ma_ref[pl.ds(pl.multiple_of(y * 8, 8), 8), pl.ds(block * 128, 128)] = packed[block]
            return carry

        lax.fori_loop(0, 4, per_y, 0)

    even = even_here()
    pl.when(even)(lambda: slab(1))
    pl.when(jnp.logical_not(even))(lambda: slab(0))


def sweep_kernel(l_ref, w_ref, g_ref, m_ref):
    zs = zspeed()
    zcoef = shares(zs)
    zforward = zs > 0.0
    for block in range(8):
        ycoef = shares(yspeed(block))
        for half in range(2):
            lanes = pl.ds(half * 1024 + block * 128, 128)
            cells = [[l_ref[pl.ds((4 * y + z) * 8, 8), lanes] for z in range(4)] for y in range(4)]
            done = sweep_yz(cells, ycoef, zcoef, zforward, block >= 4)
            for y in range(4):
                for z in range(4):
                    g_ref[pl.ds((4 * y + z) * 8, 8), lanes] = done[y][z]
    if m_ref is not None:
        m_ref[...] = weighed(w_ref, g_ref[...])


def last_sweep_kernel(l_ref, g_ref):
    sweep_kernel(l_ref, None, g_ref, None)


def sweep_edges(ra_ref, rb_ref, x_refs):
    even = jnp.full(TILE, (lax.axis_index("space") + 1) % 2, jnp.int32) > 0
    zs = zspeed()
    za, zb, zc = shares(zs)
    zforward = zs > 0.0
    for block in range(8):
        ya, yb, yc = shares(yspeed(block))
        step = -1 if block >= 4 else 1
        lanes = pl.ds(block * 128, 128)
        for half in range(2):
            cells = []
            for y in range(4):
                a, b = [r[pl.ds(y * 8, 8), lanes] for r in (ra_ref, rb_ref)]
                cells.append(jnp.where(even, b, a) if half else jnp.where(even, a, b))
            for y in range(4):
                mid = ya * cells[y] + yb * cells[(y + step) % 4] + yc * cells[(y + 2) % 4]
                near = jnp.where(zforward, pltpu.roll(mid, 2, 0), pltpu.roll(mid, 6, 0))
                x_refs[half][pl.ds(y * 8, 8), lanes] = za * mid + zb * near + zc * pltpu.roll(mid, 4, 0)


def unpacked(x_refs, y, z, half, block):
    shift = (-2 * z if half else 6 - 2 * z) % 8
    part = x_refs[half][pl.ds(y * 8, 8), pl.ds(block * 128, 128)]
    part = pltpu.roll(part, shift, 0) if shift else part
    return jnp.where(xmask(half, 1), part, jnp.zeros(TILE, jnp.float32))


def edge_kernel(g_ref, ml_ref, ra_ref, rb_ref, we_ref, o_ref, m_ref, x0_ref, x1_ref, e_ref):
    x_refs = (x0_ref, x1_ref)
    sweep_edges(ra_ref, rb_ref, x_refs)
    for y in range(4):
        for z in range(4):
            rows = pl.ds((4 * y + z) * 8, 8)
            for block in range(8):
                parts = [unpacked(x_refs, y, z, half, block) for half in range(2)]
                for half in range(2):
                    lanes = pl.ds(half * 1024 + block * 128, 128)
                    o_ref[rows, lanes] = g_ref[rows, lanes] + parts[half]
                e_ref[rows, pl.ds(block * 128, 128)] = parts[0] + parts[1]
    both = weighed(we_ref, e_ref[...])
    front = lax.broadcasted_iota(jnp.int32, (16, CELLS), 1) % LAYERS < 2
    m_ref[...] = ml_ref[...] + jnp.where(front, both[0:16, :], both[16:32, :])


def last_kernel(g_ref, ra_ref, rb_ref, o_hbm, x0_ref, x1_ref, o_ref, sems):
    x_refs = (x0_ref, x1_ref)
    sweep_edges(ra_ref, rb_ref, x_refs)
    copies = [pltpu.make_async_copy(o_ref.at[plane(y)], o_hbm.at[plane(y)], sems.at[y]) for y in range(4)]
    for y in range(4):
        for z in range(4):
            yz = 4 * y + z
            for block in range(8):
                for half in range(2):
                    value = g_ref[pl.ds(yz * 8, 8), pl.ds(half * 1024 + block * 128, 128)]
                    o_ref[:, yz * 16 + block * 2 + half, :] = value + unpacked(x_refs, y, z, half, block)
        copies[y].start()
    for copy in copies:
        copy.wait()


F32, BF16 = jnp.float32, jnp.bfloat16
HBM = pl.BlockSpec(memory_space=pl.ANY)
GRID, MESSAGE, STORED = (CELLS, 2048), (32, 1024), (LAYERS, 256, 128)
IO = [pltpu.VMEM(STORED, F32), pltpu.SemaphoreType.DMA((4,))]


def call(kernel, outs, scratch=(), hbm_in=False, hbm_out=False, **kw):
    if hbm_out:
        shapes = [jax.ShapeDtypeStruct(s, t) for s, t in outs]
    else:
        shapes = [pltpu.VMEM(s, t) for s, t in outs]

    def run(*args):
        if not hbm_in:
            args = [pltpu.with_memory_space_constraint(a, pltpu.VMEM) for a in args]
        return pl.pallas_call(
            kernel,
            out_shape=shapes,
            in_specs=[HBM if hbm_in else VMEM] * len(args),
            out_specs=[HBM if hbm_out else VMEM] * len(outs),
            scratch_shapes=list(scratch),
            **kw,
        )(*args)

    return run


def local(distribution):
    layers, breadth, height, halves, _ = distribution.shape
    vel_count = lax.axis_size("vel")
    space_count = lax.axis_size("space")
    stored = distribution.reshape(layers, breadth, height, halves, 8, 128).transpose(0, 1, 2, 4, 3, 5)
    pairs_a = [(i, i ^ 1) for i in range(space_count)]
    pairs_b = [(i, i + 1) for i in range(1, space_count - 1, 2)]
    pairs_b = pairs_b + [(j, i) for i, j in pairs_b]
    g, weights, edge_weights, partial_moments = call(
        first_kernel, [(GRID, F32), ((48, 2048), BF16), ((96, 1024), BF16), ((16, CELLS), F32)], IO, hbm_in=True
    )(stored.reshape(STORED))
    edge_scratch = [pltpu.VMEM(MESSAGE, F32), pltpu.VMEM(MESSAGE, F32)]
    for step in range(STEPS):
        everywhere = jnp.broadcast_to(partial_moments[None], (vel_count, 16, CELLS))
        gathered = lax.all_to_all(everywhere, "vel", 0, 0)
        fields, msg_b = call(outer_kernel, [((128, 128), F32), (MESSAGE, F32)])(gathered, g)
        got_b = lax.ppermute(msg_b, "space", pairs_b)
        moved, msg_a = call(inner_kernel, [(GRID, F32), (MESSAGE, F32)])(fields, g)
        got_a = lax.ppermute(msg_a, "space", pairs_a)
        if step + 1 < STEPS:
            swept, inside = call(sweep_kernel, [(GRID, F32), ((16, CELLS), F32)])(moved, weights)
            g, partial_moments = call(
                edge_kernel,
                [(GRID, F32), ((16, CELLS), F32)],
                edge_scratch + [pltpu.VMEM((CELLS, 1024), F32)],
                input_output_aliases={0: 0},
            )(swept, inside, got_a, got_b, edge_weights)
        else:
            (swept,) = call(last_sweep_kernel, [(GRID, F32)])(moved)
            (out,) = call(last_kernel, [(STORED, F32)], edge_scratch + IO, hbm_out=True)(swept, got_a, got_b)
    out = out.reshape(layers, breadth, height, 8, halves, 128).transpose(0, 1, 2, 4, 3, 5)
    return out.reshape(distribution.shape)


def solution(mesh):
    return jax.shard_map(
        local,
        mesh=mesh,
        in_specs=(P("space", None, None, None, "vel"),),
        out_specs=P("space", None, None, None, "vel"),
        check_vma=False,
    )
```

```python
import math

import jax
import jax.numpy as jnp
from jax import lax
from jax.experimental import pallas as pl
from jax.experimental.pallas import tpu as pltpu
from jax.sharding import PartitionSpec as P


NV = 32
STEPS = 3
SPEED_LIMIT = 8.0
SPACING = 2.0 * SPEED_LIMIT / NV
LAM = 1.9 / ((NV - 1) * SPEED_LIMIT / NV)
QUAD = SPACING**3 / (2.0 * math.pi) ** 1.5
LOG2E = math.log2(math.e)
LAYERS, CELLS = 8, 128
VMEM = pl.BlockSpec(memory_space=pltpu.VMEM)
TILE = (8, 128)


def iota(axis):
    return lax.broadcasted_iota(jnp.int32, TILE, axis)


def shares(speed):
    n = LAM * jnp.abs(speed)
    return (1.0 - n) * (1.0 - 0.5 * n), n * (2.0 - n), 0.5 * n * (n - 1.0)


def yspeed(block):
    return -SPEED_LIMIT + ((4 * block + iota(1) // 32).astype(jnp.float32) + 0.5) * SPACING


def zspeed():
    return -SPEED_LIMIT + ((iota(1) % 32).astype(jnp.float32) + 0.5) * SPACING


def sweep_yz(cells, ycoef, zcoef, zforward, yforward):
    step = -1 if yforward else 1
    ya, yb, yc = ycoef
    za, zb, zc = zcoef
    mid = [
        [
            ya * cells[y][z] + yb * cells[(y + step) % 4][z] + yc * cells[(y + 2) % 4][z]
            for z in range(4)
        ]
        for y in range(4)
    ]
    return [
        [
            za * mid[y][z]
            + zb * jnp.where(zforward, mid[y][(z - 1) % 4], mid[y][(z + 1) % 4])
            + zc * mid[y][(z + 2) % 4]
            for z in range(4)
        ]
        for y in range(4)
    ]


def split(x):
    high = x.astype(jnp.bfloat16)
    rest = x - high.astype(jnp.float32)
    mid = rest.astype(jnp.bfloat16)
    return high, mid, (rest - mid.astype(jnp.float32)).astype(jnp.bfloat16)


def wide(ref, rows):
    return jnp.concatenate([ref[k, rows, :] for k in range(ref.shape[0])], axis=1)


def weighed(w_ref, x):
    n = w_ref.shape[0] // 3
    total = None
    for k, part in enumerate(split(x)):
        product = lax.dot_general(
            w_ref[0 : (3 - k) * n, :], part, (((1,), (1,)), ((), ())), preferred_element_type=jnp.float32
        )
        for j in range(3 - k):
            piece = product[j * n : (j + 1) * n, :]
            total = piece if total is None else total + piece
    return total


def xabs_here():
    index = jnp.full(TILE, lax.axis_index("vel"), jnp.int32)
    return (index.astype(jnp.float32) + 0.5) * SPACING


def even_here():
    return lax.axis_index("space") % 2 == 0


def plane(y):
    return (slice(None), pl.ds(y * 64, 64), slice(None))


def first_kernel(d_hbm, g_ref, w_ref, m_ref, d_ref, sems):
    copies = [pltpu.make_async_copy(d_hbm.at[plane(y)], d_ref.at[plane(y)], sems.at[y]) for y in range(4)]
    for copy in copies:
        copy.start()
    xabs = xabs_here()
    zs = zspeed()
    row = iota(0)
    for half in range(2):
        xs = xabs if half else -xabs
        for block in range(8):
            ys = yspeed(block)
            square = xs * xs + ys * ys + zs * zs
            low = [jnp.ones_like(xs), xs, ys, zs, xs * xs, ys * ys, zs * zs, xs * ys]
            high = [xs * zs, ys * zs, xs * square, ys * square, zs * square]
            tiles = []
            for rows in (low, high):
                tile = jnp.zeros(TILE, jnp.float32)
                for i, r in enumerate(rows):
                    tile = jnp.where(row == i, r, tile)
                tiles.append(QUAD * tile)
            for k, part in enumerate(split(jnp.concatenate(tiles))):
                w_ref[pl.ds(k * 16, 16), pl.ds(half * 1024 + block * 128, 128)] = part
    for y in range(4):
        copies[y].wait()
        for z in range(4):
            yz = 4 * y + z
            for block in range(8):
                for half in range(2):
                    g_ref[half * 8 + block, pl.ds(yz * 8, 8), :] = d_ref[:, yz * 16 + block * 2 + half, :]
        m_ref[:, y * 32 : (y + 1) * 32] = weighed(w_ref, wide(g_ref, pl.ds(y * 32, 32)))


def cell_fields(m):
    rho = m[0]
    inv_rho = 1.0 / rho
    ux, uy, uz = m[1] * inv_rho, m[2] * inv_rho, m[3] * inv_rho
    energy = m[4] + m[5] + m[6]
    norm = ux * ux + uy * uy + uz * uz
    temp = (energy * inv_rho - norm) * (1.0 / 3.0)
    along = ux * m[1] + uy * m[2] + uz * m[3]

    def heating(third, u, first, r0, r1, r2):
        return 0.5 * (
            third
            - 2.0 * (ux * r0 + uy * r1 + uz * r2)
            - u * energy
            + norm * first
            + 2.0 * u * along
            - u * norm * rho
        )

    xq = heating(m[10], ux, m[1], m[4], m[7], m[8])
    yq = heating(m[11], uy, m[2], m[7], m[5], m[9])
    zq = heating(m[12], uz, m[3], m[8], m[9], m[6])
    root = jnp.sqrt(temp)
    inv_temp = 1.0 / temp
    conduction = (1.0 / 15.0) * (inv_rho * inv_temp) * inv_temp
    amp = (rho * inv_temp) * (root * inv_temp)
    retain = jnp.exp(-0.7 * rho * jnp.sqrt(root))
    k = -0.5 * LOG2E
    fold = conduction / k
    return [ux, uy, uz, k * inv_temp, fold * xq, fold * yq, fold * zq, amp * (1.0 - retain), retain]


class Cell:
    def __init__(self, tile, xabs, zs):
        (self.ux, self.uy, uz, self.scale, self.qx, self.qy, qz, self.amp, self.retain) = [
            jnp.broadcast_to(tile[:, k : k + 1], TILE) for k in range(9)
        ]
        zd = zs - uz
        self.ez, self.hz = zd * zd * self.scale, zd * qz
        self.x = []
        for xs in (-xabs, xabs):
            xd = xs - self.ux
            self.x.append((xd * xd * self.scale, xd * self.qx))

    def yz(self, block):
        yd = yspeed(block) - self.uy
        return yd * yd * self.scale + self.ez, yd * self.qy + self.hz

    def relax(self, half, yz, current):
        e = self.x[half][0] + yz[0]
        h = self.x[half][1] + yz[1]
        return self.amp * (jnp.exp2(e) * (1.0 + h * (e + 2.5 * LOG2E))) + self.retain * current


def xmask(half, far):
    row = iota(0)
    return (row < 1 + far) if half else (row > 6 - far)


def rotated(relaxed, half):
    return pltpu.roll(relaxed, 1 if half else 7, 0), pltpu.roll(relaxed, 2 if half else 6, 0)


def placed(out, half, z):
    shift = (2 * z if half else 2 * z + 2) % 8
    return pltpu.roll(out, shift, 0) if shift else out


def outer_kernel(a_ref, g_ref, f_ref, mb_ref):
    total = a_ref[0]
    for peer in range(1, a_ref.shape[0]):
        total = total + a_ref[peer]
    fields = cell_fields([total[k : k + 1, :] for k in range(13)])
    for k, value in enumerate(fields):
        f_ref[k : k + 1, :] = value
    f_ref[...] = jnp.transpose(f_ref[...])
    xabs = xabs_here()
    _, near, far = shares(xabs)
    zs = zspeed()

    def message(half):
        lower = 6 if half else 0
        near_rows = jnp.where((iota(0) < 4) if half else (iota(0) > 3), near, jnp.zeros(TILE, jnp.float32))

        def gathered(ref, y):
            return jnp.concatenate([ref[pl.ds(y * 32 + lower + layer, 4, stride=8), :] for layer in range(2)])

        for y in range(4):
            cell = Cell(gathered(f_ref, y), xabs, zs)
            for block in range(8):
                current = gathered(g_ref.at[half * 8 + block], y)
                relaxed = cell.relax(half, cell.yz(block), current)
                out = far * relaxed + near_rows * pltpu.roll(relaxed, 4, 0)
                for layer in range(2):
                    mb_ref[block, pl.ds(y * 8 + layer, 4, stride=2), :] = out[
                        layer * 4 : layer * 4 + 4, :
                    ]

    even = even_here()
    pl.when(even)(lambda: message(0))
    pl.when(jnp.logical_not(even))(lambda: message(1))


def inner_kernel(f_ref, g_ref, *refs):
    x_refs, (l_ref, ma_ref) = refs[:-2], refs[-2:]
    xabs = xabs_here()
    own, near, far = shares(xabs)
    zero = jnp.zeros(TILE, jnp.float32)
    zs = zspeed()
    inside = [
        (jnp.where(xmask(half, 0), zero, near), jnp.where(xmask(half, 1), zero, far)) for half in range(2)
    ]

    def slab(sent):
        n_out = jnp.where(xmask(sent, 0), near, zero)
        f_out = jnp.where(xmask(sent, 1), far, zero)

        def per_y(y, carry):
            packed = [zero] * 8
            for z in range(4):
                rows = pl.ds(pl.multiple_of(y * 32 + z * 8, 8), 8)
                cell = Cell(f_ref[rows, :], xabs, zs)
                for block in range(8):
                    yz = cell.yz(block)
                    for half in range(2):
                        at = half * 8 + block
                        current = g_ref[at, rows, :]
                        if x_refs:
                            current = current + unpacked(x_refs, y, z, half, block)
                        relaxed = cell.relax(half, yz, current)
                        r1, r2 = rotated(relaxed, half)
                        n_in, f_in = inside[half]
                        l_ref[at, rows, :] = own * relaxed + n_in * r1 + f_in * r2
                        if half == sent:
                            packed[block] = packed[block] + placed(n_out * r1 + f_out * r2, half, z)
            for block in range(8):
                ma_ref[block, pl.ds(pl.multiple_of(y * 8, 8), 8), :] = packed[block]
            return carry

        lax.fori_loop(0, 4, per_y, 0)

    even = even_here()
    pl.when(even)(lambda: slab(1))
    pl.when(jnp.logical_not(even))(lambda: slab(0))


def sweep_cells(l_ref, store):
    zs = zspeed()
    zcoef = shares(zs)
    zforward = zs > 0.0
    for block in range(8):
        ycoef = shares(yspeed(block))
        for half in range(2):
            cells = [[l_ref[half * 8 + block, pl.ds((4 * y + z) * 8, 8), :] for z in range(4)] for y in range(4)]
            done = sweep_yz(cells, ycoef, zcoef, zforward, block >= 4)
            for y in range(4):
                for z in range(4):
                    store(4 * y + z, half, block, done[y][z])


def sweep_kernel(l_ref, w_ref, g_ref, m_ref):
    def store(yz, half, block, value):
        g_ref[half * 8 + block, pl.ds(yz * 8, 8), :] = value

    sweep_cells(l_ref, store)
    m_ref[...] = weighed(w_ref, wide(g_ref, slice(None)))


def last_sweep_kernel(l_ref, o_ref):
    def store(yz, half, block, value):
        o_ref[:, yz * 16 + block * 2 + half, :] = value

    sweep_cells(l_ref, store)


def sweep_edges(ra_ref, rb_ref, x_refs):
    even = jnp.full(TILE, (lax.axis_index("space") + 1) % 2, jnp.int32) > 0
    zs = zspeed()
    za, zb, zc = shares(zs)
    zforward = zs > 0.0
    for block in range(8):
        ya, yb, yc = shares(yspeed(block))
        step = -1 if block >= 4 else 1
        for half in range(2):
            cells = []
            for y in range(4):
                a, b = [r[block, pl.ds(y * 8, 8), :] for r in (ra_ref, rb_ref)]
                cells.append(jnp.where(even, b, a) if half else jnp.where(even, a, b))
            for y in range(4):
                mid = ya * cells[y] + yb * cells[(y + step) % 4] + yc * cells[(y + 2) % 4]
                near = jnp.where(zforward, pltpu.roll(mid, 2, 0), pltpu.roll(mid, 6, 0))
                x_refs[half][block, pl.ds(y * 8, 8), :] = za * mid + zb * near + zc * pltpu.roll(mid, 4, 0)


def unpacked(x_refs, y, z, half, block):
    shift = (-2 * z if half else 6 - 2 * z) % 8
    part = x_refs[half][block, pl.ds(pl.multiple_of(y * 8, 8), 8), :]
    part = pltpu.roll(part, shift, 0) if shift else part
    return jnp.where(xmask(half, 1), part, jnp.zeros(TILE, jnp.float32))


def edge_kernel(ml_ref, ra_ref, rb_ref, w_ref, x0_ref, x1_ref, m_ref):
    x_refs = (x0_ref, x1_ref)
    sweep_edges(ra_ref, rb_ref, x_refs)
    total = ml_ref[...]
    source = lax.broadcasted_iota(jnp.int32, (32, CELLS), 0)
    cell = lax.broadcasted_iota(jnp.int32, (32, CELLS), 1)
    for half in range(2):
        sums = weighed(w_ref.at[:, pl.ds(half * 1024, 1024)], wide(x_refs[half], slice(None)))
        target = source // 2 * 8 + source % 2 + (0 if half else 6)
        spread = (target == cell).astype(jnp.bfloat16)
        for part in split(sums):
            total = total + jnp.dot(part, spread, preferred_element_type=jnp.float32)
    m_ref[...] = total


def last_kernel(s_ref, ra_ref, rb_ref, o_hbm, x0_ref, x1_ref, e_ref, sems):
    inside = pltpu.make_async_copy(s_ref.at[pl.ds(2, 4)], o_hbm.at[pl.ds(2, 4)], sems.at[4])
    inside.start()
    x_refs = (x0_ref, x1_ref)
    sweep_edges(ra_ref, rb_ref, x_refs)
    copies = []
    for half in (1, 0):
        for layer in range(2):
            at = layer if half else 2 + layer
            outer = layer if half else 6 + layer
            e_ref[at] = s_ref[outer]
            for y in range(4):
                for block in range(8):
                    rows = pl.ds(y * 64 + block * 2 + half, 4, stride=16)
                    part = x_refs[half][block, pl.ds(y * 8 + layer, 4, stride=2), :]
                    e_ref[at, rows, :] = e_ref[at, rows, :] + part
            copies.append(pltpu.make_async_copy(e_ref.at[at], o_hbm.at[outer], sems.at[at]))
            copies[-1].start()
    for copy in [inside] + copies:
        copy.wait()


F32, BF16 = jnp.float32, jnp.bfloat16
HBM = pl.BlockSpec(memory_space=pltpu.HBM)
GRID, MESSAGE, STORED = (16, CELLS, 128), (8, 32, 128), (LAYERS, 256, 128)
EDGES = [pltpu.VMEM(MESSAGE, F32), pltpu.VMEM(MESSAGE, F32)]


def call(kernel, outs, scratch=(), hbm_in=False, hbm_out=False, **kw):
    if hbm_out:
        shapes = [jax.ShapeDtypeStruct(s, t) for s, t in outs]
    else:
        shapes = [pltpu.VMEM(s, t) for s, t in outs]

    def run(*args):
        space = pltpu.HBM if hbm_in else pltpu.VMEM
        args = [pltpu.with_memory_space_constraint(a, space) for a in args]
        return pl.pallas_call(
            kernel,
            out_shape=shapes,
            in_specs=[HBM if hbm_in else VMEM] * len(args),
            out_specs=[HBM if hbm_out else VMEM] * len(outs),
            scratch_shapes=list(scratch),
            compiler_params=pltpu.CompilerParams(vmem_limit_bytes=8 << 20),
            **kw,
        )(*args)

    return run


def local(distribution):
    layers, breadth, height, halves, _ = distribution.shape
    vel_count = lax.axis_size("vel")
    space_count = lax.axis_size("space")
    stored = distribution.reshape(layers, breadth, height, halves, 8, 128).transpose(0, 1, 2, 4, 3, 5)
    pairs_a = [(i, i ^ 1) for i in range(space_count)]
    pairs_b = [(i, i + 1) for i in range(1, space_count - 1, 2)]
    pairs_b = pairs_b + [(j, i) for i, j in pairs_b]
    g, weights, partial_moments = call(
        first_kernel,
        [(GRID, F32), ((48, 2048), BF16), ((16, CELLS), F32)],
        [pltpu.VMEM(STORED, F32), pltpu.SemaphoreType.DMA((4,))],
        hbm_in=True,
    )(stored.reshape(STORED))
    sides = ()
    for step in range(STEPS):
        everywhere = jnp.broadcast_to(partial_moments[None], (vel_count, 16, CELLS))
        gathered = lax.all_to_all(everywhere, "vel", 0, 0)
        fields, msg_b = call(outer_kernel, [((128, 128), F32), (MESSAGE, F32)])(gathered, g)
        got_b = lax.ppermute(msg_b, "space", pairs_b)
        moved, msg_a = call(inner_kernel, [(GRID, F32), (MESSAGE, F32)])(fields, g, *sides)
        got_a = lax.ppermute(msg_a, "space", pairs_a)
        if step + 1 < STEPS:
            g, inside = call(sweep_kernel, [(GRID, F32), ((16, CELLS), F32)])(
                moved, weights
            )
            *sides, partial_moments = call(
                edge_kernel, [(MESSAGE, F32), (MESSAGE, F32), ((16, CELLS), F32)]
            )(inside, got_a, got_b, weights)
        else:
            (swept,) = call(last_sweep_kernel, [(STORED, F32)])(moved)
            (out,) = call(
                last_kernel,
                [(STORED, F32)],
                EDGES + [pltpu.VMEM((4, 256, 128), F32), pltpu.SemaphoreType.DMA((5,))],
                hbm_out=True,
            )(swept, got_a, got_b)
    out = out.reshape(layers, breadth, height, 8, halves, 128).transpose(0, 1, 2, 4, 3, 5)
    return out.reshape(distribution.shape)


def solution(mesh):
    return jax.shard_map(
        local,
        mesh=mesh,
        in_specs=(P("space", None, None, None, "vel"),),
        out_specs=P("space", None, None, None, "vel"),
        check_vma=False,
    )
```

```python
import math

import jax
import jax.numpy as jnp
from jax import lax
from jax.experimental import pallas as pl
from jax.experimental.pallas import tpu as pltpu
from jax.sharding import PartitionSpec as P


NV = 32
STEPS = 3
SPEED_LIMIT = 8.0
SPACING = 2.0 * SPEED_LIMIT / NV
LAM = 1.9 / ((NV - 1) * SPEED_LIMIT / NV)
QUAD = SPACING**3 / (2.0 * math.pi) ** 1.5
LOG2E = math.log2(math.e)
LAYERS, CELLS = 8, 128
VMEM = pl.BlockSpec(memory_space=pltpu.VMEM)
TILE = (8, 128)


def iota(axis):
    return lax.broadcasted_iota(jnp.int32, TILE, axis)


def shares(speed):
    n = LAM * jnp.abs(speed)
    return (1.0 - n) * (1.0 - 0.5 * n), n * (2.0 - n), 0.5 * n * (n - 1.0)


def yspeed(block):
    return -SPEED_LIMIT + ((4 * block + iota(1) // 32).astype(jnp.float32) + 0.5) * SPACING


def zspeed():
    return -SPEED_LIMIT + ((iota(1) % 32).astype(jnp.float32) + 0.5) * SPACING


def sweep_yz(cells, ycoef, zcoef, zforward, yforward):
    step = -1 if yforward else 1
    ya, yb, yc = ycoef
    za, zb, zc = zcoef
    mid = [
        [
            ya * cells[y][z] + yb * cells[(y + step) % 4][z] + yc * cells[(y + 2) % 4][z]
            for z in range(4)
        ]
        for y in range(4)
    ]
    return [
        [
            za * mid[y][z]
            + zb * jnp.where(zforward, mid[y][(z - 1) % 4], mid[y][(z + 1) % 4])
            + zc * mid[y][(z + 2) % 4]
            for z in range(4)
        ]
        for y in range(4)
    ]


def split(x):
    high = x.astype(jnp.bfloat16)
    rest = x - high.astype(jnp.float32)
    mid = rest.astype(jnp.bfloat16)
    return high, mid, (rest - mid.astype(jnp.float32)).astype(jnp.bfloat16)


def wide(ref, rows):
    return jnp.concatenate([ref[k, rows, :] for k in range(ref.shape[0])], axis=1)


def weighed(w_ref, x):
    n = w_ref.shape[0] // 3
    total = None
    for k, part in enumerate(split(x)):
        product = lax.dot_general(
            w_ref[0 : (3 - k) * n, :], part, (((1,), (1,)), ((), ())), preferred_element_type=jnp.float32
        )
        for j in range(3 - k):
            piece = product[j * n : (j + 1) * n, :]
            total = piece if total is None else total + piece
    return total


def xabs_here():
    index = jnp.full(TILE, lax.axis_index("vel"), jnp.int32)
    return (index.astype(jnp.float32) + 0.5) * SPACING


def even_here():
    return lax.axis_index("space") % 2 == 0


def first_kernel(d_hbm, g_ref, w_ref, m_ref, d_ref, sems):
    copies = []
    for k in range(8):
        part = (slice(None), pl.ds(k * 32, 32), slice(None))
        copies.append(pltpu.make_async_copy(d_hbm.at[part], d_ref.at[part], sems.at[k]))
    for copy in copies:
        copy.start()
    xabs = xabs_here()
    zs = zspeed()
    row = iota(0)
    for half in range(2):
        xs = xabs if half else -xabs
        for block in range(8):
            ys = yspeed(block)
            square = xs * xs + ys * ys + zs * zs
            low = [jnp.ones_like(xs), xs, ys, zs, xs * xs, ys * ys, zs * zs, xs * ys]
            high = [xs * zs, ys * zs, xs * square, ys * square, zs * square]
            tiles = []
            for rows in (low, high):
                tile = jnp.zeros(TILE, jnp.float32)
                for i, r in enumerate(rows):
                    tile = jnp.where(row == i, r, tile)
                tiles.append(QUAD * tile)
            for k, part in enumerate(split(jnp.concatenate(tiles))):
                w_ref[pl.ds(k * 16, 16), pl.ds(half * 1024 + block * 128, 128)] = part
    for k in range(8):
        copies[k].wait()
        for yz in (2 * k, 2 * k + 1):
            for block in range(8):
                for half in range(2):
                    g_ref[half * 8 + block, pl.ds(yz * 8, 8), :] = d_ref[:, yz * 16 + block * 2 + half, :]
    m_ref[...] = weighed(w_ref, wide(g_ref, slice(None)))


def cell_fields(m):
    rho = m[0]
    inv_rho = 1.0 / rho
    ux, uy, uz = m[1] * inv_rho, m[2] * inv_rho, m[3] * inv_rho
    energy = m[4] + m[5] + m[6]
    norm = ux * ux + uy * uy + uz * uz
    temp = (energy * inv_rho - norm) * (1.0 / 3.0)
    along = ux * m[1] + uy * m[2] + uz * m[3]

    def heating(third, u, first, r0, r1, r2):
        return 0.5 * (
            third
            - 2.0 * (ux * r0 + uy * r1 + uz * r2)
            - u * energy
            + norm * first
            + 2.0 * u * along
            - u * norm * rho
        )

    xq = heating(m[10], ux, m[1], m[4], m[7], m[8])
    yq = heating(m[11], uy, m[2], m[7], m[5], m[9])
    zq = heating(m[12], uz, m[3], m[8], m[9], m[6])
    root = jnp.sqrt(temp)
    inv_temp = 1.0 / temp
    conduction = (1.0 / 15.0) * (inv_rho * inv_temp) * inv_temp
    amp = (rho * inv_temp) * (root * inv_temp)
    retain = jnp.exp(-0.7 * rho * jnp.sqrt(root))
    k = -0.5 * LOG2E
    fold = conduction / k
    return [ux, uy, uz, k * inv_temp, fold * xq, fold * yq, fold * zq, amp * (1.0 - retain), retain]


class Cell:
    def __init__(self, tile, xabs, zs):
        (self.ux, self.uy, uz, self.scale, self.qx, self.qy, qz, self.amp, self.retain) = [
            jnp.broadcast_to(tile[:, k : k + 1], TILE) for k in range(9)
        ]
        zd = zs - uz
        self.ez, self.hz = zd * zd * self.scale, zd * qz
        self.x = []
        for xs in (-xabs, xabs):
            xd = xs - self.ux
            self.x.append((xd * xd * self.scale, xd * self.qx))

    def yz(self, block):
        yd = yspeed(block) - self.uy
        return yd * yd * self.scale + self.ez, yd * self.qy + self.hz

    def relax(self, half, yz, current):
        e = self.x[half][0] + yz[0]
        h = self.x[half][1] + yz[1]
        return self.amp * (jnp.exp2(e) * (1.0 + h * (e + 2.5 * LOG2E))) + self.retain * current


def xmask(half, far):
    row = iota(0)
    return (row < 1 + far) if half else (row > 6 - far)


def rotated(relaxed, half):
    return pltpu.roll(relaxed, 1 if half else 7, 0), pltpu.roll(relaxed, 2 if half else 6, 0)


def placed(out, half, z):
    shift = (2 * z if half else 2 * z + 2) % 8
    return pltpu.roll(out, shift, 0) if shift else out


def outer_kernel(a_ref, g_ref, f_ref, mb_ref):
    total = a_ref[0]
    for peer in range(1, a_ref.shape[0]):
        total = total + a_ref[peer]
    fields = cell_fields([total[k : k + 1, :] for k in range(13)])
    for k, value in enumerate(fields):
        f_ref[k : k + 1, :] = value
    f_ref[...] = jnp.transpose(f_ref[...])
    xabs = xabs_here()
    _, near, far = shares(xabs)
    zs = zspeed()

    def message(half):
        lower = 6 if half else 0
        near_rows = jnp.where((iota(0) < 4) if half else (iota(0) > 3), near, jnp.zeros(TILE, jnp.float32))

        def gathered(ref, y):
            return jnp.concatenate([ref[pl.ds(y * 32 + lower + layer, 4, stride=8), :] for layer in range(2)])

        for y in range(4):
            cell = Cell(gathered(f_ref, y), xabs, zs)
            for block in range(8):
                current = gathered(g_ref.at[half * 8 + block], y)
                relaxed = cell.relax(half, cell.yz(block), current)
                out = far * relaxed + near_rows * pltpu.roll(relaxed, 4, 0)
                for layer in range(2):
                    mb_ref[block, pl.ds(y * 8 + layer, 4, stride=2), :] = out[
                        layer * 4 : layer * 4 + 4, :
                    ]

    even = even_here()
    pl.when(even)(lambda: message(0))
    pl.when(jnp.logical_not(even))(lambda: message(1))


def inner_kernel(f_ref, g_ref, *refs):
    sides, (l_ref, ma_ref) = refs[:-2], refs[-2:]
    xabs = xabs_here()
    own, near, far = shares(xabs)
    zero = jnp.zeros(TILE, jnp.float32)
    zs = zspeed()
    inside = [
        (jnp.where(xmask(half, 0), zero, near), jnp.where(xmask(half, 1), zero, far)) for half in range(2)
    ]

    def slab(sent):
        x_refs = sides if sent else sides[::-1]
        n_out = jnp.where(xmask(sent, 0), near, zero)
        f_out = jnp.where(xmask(sent, 1), far, zero)

        def per_y(y, carry):
            packed = [zero] * 8
            for z in range(4):
                rows = pl.ds(pl.multiple_of(y * 32 + z * 8, 8), 8)
                cell = Cell(f_ref[rows, :], xabs, zs)
                for block in range(8):
                    yz = cell.yz(block)
                    for half in range(2):
                        at = half * 8 + block
                        current = g_ref[at, rows, :]
                        if x_refs:
                            current = current + unpacked(x_refs, y, z, half, block)
                        relaxed = cell.relax(half, yz, current)
                        r1, r2 = rotated(relaxed, half)
                        n_in, f_in = inside[half]
                        l_ref[at, rows, :] = own * relaxed + n_in * r1 + f_in * r2
                        if half == sent:
                            packed[block] = packed[block] + placed(n_out * r1 + f_out * r2, half, z)
            for block in range(8):
                ma_ref[block, pl.ds(pl.multiple_of(y * 8, 8), 8), :] = packed[block]
            return carry

        lax.fori_loop(0, 4, per_y, 0)

    even = even_here()
    pl.when(even)(lambda: slab(1))
    pl.when(jnp.logical_not(even))(lambda: slab(0))


def sweep_cells(l_ref, store):
    zs = zspeed()
    zcoef = shares(zs)
    zforward = zs > 0.0
    for block in range(8):
        ycoef = shares(yspeed(block))
        for half in range(2):
            cells = [[l_ref[half * 8 + block, pl.ds((4 * y + z) * 8, 8), :] for z in range(4)] for y in range(4)]
            done = sweep_yz(cells, ycoef, zcoef, zforward, block >= 4)
            for y in range(4):
                for z in range(4):
                    store(4 * y + z, half, block, done[y][z])


def sweep_kernel(l_ref, w_ref, g_ref, m_ref):
    def store(yz, half, block, value):
        g_ref[half * 8 + block, pl.ds(yz * 8, 8), :] = value

    sweep_cells(l_ref, store)
    m_ref[...] = weighed(w_ref, wide(g_ref, slice(None)))


def last_sweep_kernel(l_ref, o_ref):
    def store(yz, half, block, value):
        o_ref[:, yz * 16 + block * 2 + half, :] = value

    sweep_cells(l_ref, store)


def sweep_edges(ra_ref, rb_ref, x_refs):
    even = jnp.full(TILE, (lax.axis_index("space") + 1) % 2, jnp.int32) > 0
    zs = zspeed()
    za, zb, zc = shares(zs)
    zforward = zs > 0.0
    for block in range(8):
        ya, yb, yc = shares(yspeed(block))
        step = -1 if block >= 4 else 1
        for half in range(2):
            cells = []
            for y in range(4):
                a, b = [r[block, pl.ds(y * 8, 8), :] for r in (ra_ref, rb_ref)]
                cells.append(jnp.where(even, b, a) if half else jnp.where(even, a, b))
            for y in range(4):
                mid = ya * cells[y] + yb * cells[(y + step) % 4] + yc * cells[(y + 2) % 4]
                near = jnp.where(zforward, pltpu.roll(mid, 2, 0), pltpu.roll(mid, 6, 0))
                x_refs[half][block, pl.ds(y * 8, 8), :] = za * mid + zb * near + zc * pltpu.roll(mid, 4, 0)


def unpacked(x_refs, y, z, half, block):
    shift = (-2 * z if half else 6 - 2 * z) % 8
    part = x_refs[half][block, pl.ds(pl.multiple_of(y * 8, 8), 8), :]
    part = pltpu.roll(part, shift, 0) if shift else part
    return jnp.where(xmask(half, 1), part, jnp.zeros(TILE, jnp.float32))


def edge_kernel(half, mi_ref, r_ref, w_ref, x_ref, m_ref):
    zs = zspeed()
    za, zb, zc = shares(zs)
    zforward = zs > 0.0
    for block in range(8):
        ya, yb, yc = shares(yspeed(block))
        step = -1 if block >= 4 else 1
        cells = [r_ref[block, pl.ds(y * 8, 8), :] for y in range(4)]
        for y in range(4):
            mid = ya * cells[y] + yb * cells[(y + step) % 4] + yc * cells[(y + 2) % 4]
            near = jnp.where(zforward, pltpu.roll(mid, 2, 0), pltpu.roll(mid, 6, 0))
            x_ref[block, pl.ds(y * 8, 8), :] = za * mid + zb * near + zc * pltpu.roll(mid, 4, 0)
    at = pl.ds(pl.multiple_of(half * 1024, 1024), 1024)
    sums = weighed(w_ref.at[:, at], wide(x_ref, slice(None)))
    source = lax.broadcasted_iota(jnp.int32, (32, CELLS), 0)
    cell = lax.broadcasted_iota(jnp.int32, (32, CELLS), 1)
    spread = (source // 2 * 8 + source % 2 + 6 * (1 - half) == cell).astype(jnp.bfloat16)
    thirds = jnp.dot(jnp.concatenate(split(sums)), spread, preferred_element_type=jnp.float32)
    m_ref[...] = mi_ref[...] + ((thirds[32:48, :] + thirds[16:32, :]) + thirds[0:16, :])


def chip_edge_kernel(*refs):
    edge_kernel(lax.axis_index("space") % 2, *refs)


def far_edge_kernel(*refs):
    edge_kernel(1 - lax.axis_index("space") % 2, *refs)


def last_kernel(s_ref, ra_ref, rb_ref, o_hbm, x0_ref, x1_ref, e_ref, sems):
    inside = pltpu.make_async_copy(s_ref.at[pl.ds(2, 4), pl.ds(0, 256)], o_hbm.at[pl.ds(2, 4)], sems.at[4])
    inside.start()
    x_refs = (x0_ref, x1_ref)
    sweep_edges(ra_ref, rb_ref, x_refs)
    copies = []
    for half in (1, 0):
        for layer in range(2):
            at = layer if half else 2 + layer
            outer = layer if half else 6 + layer
            e_ref[at] = s_ref[outer, 0:256, :]
            for y in range(4):
                for block in range(8):
                    rows = pl.ds(y * 64 + block * 2 + half, 4, stride=16)
                    part = x_refs[half][block, pl.ds(y * 8 + layer, 4, stride=2), :]
                    e_ref[at, rows, :] = e_ref[at, rows, :] + part
            copies.append(pltpu.make_async_copy(e_ref.at[at], o_hbm.at[outer], sems.at[at]))
            copies[-1].start()
    for copy in [inside] + copies:
        copy.wait()


F32, BF16 = jnp.float32, jnp.bfloat16
HBM = pl.BlockSpec(memory_space=pltpu.HBM)
GRID, MESSAGE, STORED = (16, CELLS, 128), (8, 32, 128), (LAYERS, 256, 128)
PADDED = (LAYERS, 264, 128)
EDGES = [pltpu.VMEM(MESSAGE, F32), pltpu.VMEM(MESSAGE, F32)]


def call(kernel, outs, scratch=(), hbm_in=False, hbm_out=False, **kw):
    if hbm_out:
        shapes = [jax.ShapeDtypeStruct(s, t) for s, t in outs]
    else:
        shapes = [pltpu.VMEM(s, t) for s, t in outs]

    def run(*args):
        space = pltpu.HBM if hbm_in else pltpu.VMEM
        args = [pltpu.with_memory_space_constraint(a, space) for a in args]
        return pl.pallas_call(
            kernel,
            out_shape=shapes,
            in_specs=[HBM if hbm_in else VMEM] * len(args),
            out_specs=[HBM if hbm_out else VMEM] * len(outs),
            scratch_shapes=list(scratch),
            compiler_params=pltpu.CompilerParams(vmem_limit_bytes=8 << 20),
            **kw,
        )(*args)

    return run


def local(distribution):
    layers, breadth, height, halves, _ = distribution.shape
    vel_count = lax.axis_size("vel")
    space_count = lax.axis_size("space")
    stored = distribution.reshape(layers, breadth, height, halves, 8, 128).transpose(0, 1, 2, 4, 3, 5)
    pairs_a = [(i, i ^ 1) for i in range(space_count)]
    pairs_b = [(i, i + 1) for i in range(1, space_count - 1, 2)]
    pairs_b = pairs_b + [(j, i) for i, j in pairs_b]
    g, weights, partial_moments = call(
        first_kernel,
        [(GRID, F32), ((48, 2048), BF16), ((16, CELLS), F32)],
        [pltpu.VMEM(PADDED, F32), pltpu.SemaphoreType.DMA((8,))],
        hbm_in=True,
    )(stored.reshape(STORED))
    sides = ()
    for step in range(STEPS):
        everywhere = jnp.broadcast_to(partial_moments[None], (vel_count, 16, CELLS))
        gathered = lax.all_to_all(everywhere, "vel", 0, 0)
        fields, msg_b = call(outer_kernel, [((128, 128), F32), (MESSAGE, F32)])(gathered, g)
        got_b = lax.ppermute(msg_b, "space", pairs_b)
        moved, msg_a = call(inner_kernel, [(GRID, F32), (MESSAGE, F32)])(fields, g, *sides)
        got_a = lax.ppermute(msg_a, "space", pairs_a)
        if step + 1 < STEPS:
            g, inside = call(sweep_kernel, [(GRID, F32), ((16, CELLS), F32)])(
                moved, weights
            )
            outs = [(MESSAGE, F32), ((16, CELLS), F32)]
            near, inside = call(chip_edge_kernel, outs)(inside, got_a, weights)
            distant, partial_moments = call(far_edge_kernel, outs)(inside, got_b, weights)
            sides = (near, distant)
        else:
            (swept,) = call(last_sweep_kernel, [(PADDED, F32)])(moved)
            (out,) = call(
                last_kernel,
                [(STORED, F32)],
                EDGES + [pltpu.VMEM((4, 256, 128), F32), pltpu.SemaphoreType.DMA((5,))],
                hbm_out=True,
            )(swept, got_a, got_b)
    out = out.reshape(layers, breadth, height, 8, halves, 128).transpose(0, 1, 2, 4, 3, 5)
    return out.reshape(distribution.shape)


def solution(mesh):
    return jax.shard_map(
        local,
        mesh=mesh,
        in_specs=(P("space", None, None, None, "vel"),),
        out_specs=P("space", None, None, None, "vel"),
        check_vma=False,
    )
```

```python
import math

import jax
import jax.numpy as jnp
from jax import lax
from jax.experimental import pallas as pl
from jax.experimental.pallas import tpu as pltpu
from jax.sharding import PartitionSpec as P


NV = 32
STEPS = 3
SPEED_LIMIT = 8.0
SPACING = 2.0 * SPEED_LIMIT / NV
LAM = 1.9 / ((NV - 1) * SPEED_LIMIT / NV)
QUAD = SPACING**3 / (2.0 * math.pi) ** 1.5
LOG2E = math.log2(math.e)
LAYERS, NYZ, CELLS = 8, 16, 128
VMEM = pl.BlockSpec(memory_space=pltpu.VMEM)
TILE = (8, 128)


def iota(axis):
    return lax.broadcasted_iota(jnp.int32, TILE, axis)


def shares(speed):
    n = LAM * jnp.abs(speed)
    return (1.0 - n) * (1.0 - 0.5 * n), n * (2.0 - n), 0.5 * n * (n - 1.0)


def yspeed(block):
    return -SPEED_LIMIT + ((4 * block + iota(1) // 32).astype(jnp.float32) + 0.5) * SPACING


def zspeed():
    return -SPEED_LIMIT + ((iota(1) % 32).astype(jnp.float32) + 0.5) * SPACING


def sweep_yz(cells, ycoef, zcoef, zforward, yforward):
    step = -1 if yforward else 1
    ya, yb, yc = ycoef
    za, zb, zc = zcoef
    mid = [
        [
            ya * cells[y][z] + yb * cells[(y + step) % 4][z] + yc * cells[(y + 2) % 4][z]
            for z in range(4)
        ]
        for y in range(4)
    ]
    return [
        [
            za * mid[y][z]
            + zb * jnp.where(zforward, mid[y][(z - 1) % 4], mid[y][(z + 1) % 4])
            + zc * mid[y][(z + 2) % 4]
            for z in range(4)
        ]
        for y in range(4)
    ]


def split(x):
    high = x.astype(jnp.bfloat16)
    rest = x - high.astype(jnp.float32)
    mid = rest.astype(jnp.bfloat16)
    return high, mid, (rest - mid.astype(jnp.float32)).astype(jnp.bfloat16)


def wide(ref, rows):
    return jnp.concatenate([ref[k, rows, :] for k in range(ref.shape[0])], axis=1)


def weighed(w_ref, x):
    n = w_ref.shape[0] // 3
    total = None
    for k, part in enumerate(split(x)):
        product = lax.dot_general(
            w_ref[0 : (3 - k) * n, :], part, (((1,), (1,)), ((), ())), preferred_element_type=jnp.float32
        )
        for j in range(3 - k):
            piece = product[j * n : (j + 1) * n, :]
            total = piece if total is None else total + piece
    return total


def xabs_here():
    index = jnp.full(TILE, lax.axis_index("vel"), jnp.int32)
    return (index.astype(jnp.float32) + 0.5) * SPACING


def even_here():
    return lax.axis_index("space") % 2 == 0


def first_kernel(d_hbm, g_ref, w_ref, m_ref, d_ref, sems):
    copies = []
    for k in range(8):
        part = (slice(None), pl.ds(k * 32, 32), slice(None))
        copies.append(pltpu.make_async_copy(d_hbm.at[part], d_ref.at[part], sems.at[k]))
    for copy in copies:
        copy.start()
    xabs = xabs_here()
    zs = zspeed()
    row = iota(0)
    for half in range(2):
        xs = xabs if half else -xabs
        for block in range(8):
            ys = yspeed(block)
            square = xs * xs + ys * ys + zs * zs
            low = [jnp.ones_like(xs), xs, ys, zs, xs * xs, ys * ys, zs * zs, xs * ys]
            high = [xs * zs, ys * zs, xs * square, ys * square, zs * square]
            tiles = []
            for rows in (low, high):
                tile = jnp.zeros(TILE, jnp.float32)
                for i, r in enumerate(rows):
                    tile = jnp.where(row == i, r, tile)
                tiles.append(QUAD * tile)
            for k, part in enumerate(split(jnp.concatenate(tiles))):
                w_ref[pl.ds(k * 16, 16), pl.ds(half * 1024 + block * 128, 128)] = part
    for k in range(8):
        copies[k].wait()
        for yz in (2 * k, 2 * k + 1):
            for group in range(2):
                turned = jnp.swapaxes(d_ref[:, pl.ds(yz * 16 + group * 8, 8), :], 0, 1)
                for k in range(8):
                    block, half = group * 4 + k // 2, k % 2
                    g_ref[half * 8 + block, pl.ds(yz * 8, 8), :] = turned[k]
    m_ref[...] = jnp.broadcast_to(weighed(w_ref, wide(g_ref, slice(None)))[None], m_ref.shape)


def cell_fields(m):
    rho = m[0]
    inv_rho = 1.0 / rho
    ux, uy, uz = m[1] * inv_rho, m[2] * inv_rho, m[3] * inv_rho
    energy = m[4] + m[5] + m[6]
    norm = ux * ux + uy * uy + uz * uz
    temp = (energy * inv_rho - norm) * (1.0 / 3.0)
    along = ux * m[1] + uy * m[2] + uz * m[3]

    def heating(third, u, first, r0, r1, r2):
        return 0.5 * (
            third
            - 2.0 * (ux * r0 + uy * r1 + uz * r2)
            - u * energy
            + norm * first
            + 2.0 * u * along
            - u * norm * rho
        )

    xq = heating(m[10], ux, m[1], m[4], m[7], m[8])
    yq = heating(m[11], uy, m[2], m[7], m[5], m[9])
    zq = heating(m[12], uz, m[3], m[8], m[9], m[6])
    root = jnp.sqrt(temp)
    inv_temp = 1.0 / temp
    conduction = (1.0 / 15.0) * (inv_rho * inv_temp) * inv_temp
    amp = (rho * inv_temp) * (root * inv_temp)
    retain = jnp.exp(-0.7 * rho * jnp.sqrt(root))
    k = -0.5 * LOG2E
    fold = conduction / k
    return [ux, uy, uz, k * inv_temp, fold * xq, fold * yq, fold * zq, amp * (1.0 - retain), retain]


class Cell:
    def __init__(self, tile, xabs, zs):
        (self.ux, self.uy, uz, self.scale, self.qx, self.qy, qz, self.amp, self.retain) = [
            jnp.broadcast_to(tile[:, k : k + 1], TILE) for k in range(9)
        ]
        zd = zs - uz
        self.ez, self.hz = zd * zd * self.scale, zd * qz
        self.x = []
        for xs in (-xabs, xabs):
            xd = xs - self.ux
            self.x.append((xd * xd * self.scale, xd * self.qx))

    def yz(self, block):
        yd = yspeed(block) - self.uy
        return yd * yd * self.scale + self.ez, yd * self.qy + self.hz

    def relax(self, half, yz, current):
        e = self.x[half][0] + yz[0]
        h = self.x[half][1] + yz[1]
        return self.amp * (jnp.exp2(e) * (1.0 + h * (e + 2.5 * LOG2E))) + self.retain * current


def xmask(half, far):
    row = iota(0)
    return (row < 1 + far) if half else (row > 6 - far)


def rotated(relaxed, half):
    return pltpu.roll(relaxed, 1 if half else 7, 0), pltpu.roll(relaxed, 2 if half else 6, 0)


def placed(out, half, z):
    shift = (2 * z if half else 2 * z + 2) % 8
    return pltpu.roll(out, shift, 0) if shift else out


def outer_kernel(a_ref, g_ref, f_ref, mb_ref):
    total = a_ref[0]
    for peer in range(1, a_ref.shape[0]):
        total = total + a_ref[peer]
    fields = cell_fields([total[k : k + 1, :] for k in range(13)])
    for k, value in enumerate(fields):
        f_ref[k : k + 1, :] = value
    f_ref[...] = jnp.transpose(f_ref[...])
    xabs = xabs_here()
    _, near, far = shares(xabs)
    zs = zspeed()

    def message(half):
        lower = 6 if half else 0
        near_rows = jnp.where((iota(0) < 4) if half else (iota(0) > 3), near, jnp.zeros(TILE, jnp.float32))

        def gathered(ref, y):
            return jnp.concatenate([ref[pl.ds(y * 32 + lower + layer, 4, stride=8), :] for layer in range(2)])

        for y in range(4):
            cell = Cell(gathered(f_ref, y), xabs, zs)
            for block in range(8):
                current = gathered(g_ref.at[half * 8 + block], y)
                relaxed = cell.relax(half, cell.yz(block), current)
                out = far * relaxed + near_rows * pltpu.roll(relaxed, 4, 0)
                for layer in range(2):
                    mb_ref[block, pl.ds(y * 8 + layer, 4, stride=2), :] = out[
                        layer * 4 : layer * 4 + 4, :
                    ]

    even = even_here()
    pl.when(even)(lambda: message(0))
    pl.when(jnp.logical_not(even))(lambda: message(1))


def inner_kernel(f_ref, g_ref, sides, l_ref, ma_ref, on_even):
    xabs = xabs_here()
    own, near, far = shares(xabs)
    zero = jnp.zeros(TILE, jnp.float32)
    zs = zspeed()
    inside = [
        (jnp.where(xmask(half, 0), zero, near), jnp.where(xmask(half, 1), zero, far)) for half in range(2)
    ]

    def slab(sent):
        x_refs = sides if sent else sides[::-1]
        n_out = jnp.where(xmask(sent, 0), near, zero)
        f_out = jnp.where(xmask(sent, 1), far, zero)

        def per_y(y, carry):
            packed = [zero] * 8
            for z in range(4):
                rows = pl.ds(pl.multiple_of(y * 32 + z * 8, 8), 8)
                cell = Cell(f_ref[rows, :], xabs, zs)
                for block in range(8):
                    yz = cell.yz(block)
                    for half in range(2):
                        at = half * 8 + block
                        current = g_ref[at, rows, :]
                        if x_refs:
                            current = current + unpacked(x_refs, y, z, half, block)
                        relaxed = cell.relax(half, yz, current)
                        r1, r2 = rotated(relaxed, half)
                        n_in, f_in = inside[half]
                        l_ref[at, rows, :] = own * relaxed + n_in * r1 + f_in * r2
                        if half == sent:
                            packed[block] = packed[block] + placed(n_out * r1 + f_out * r2, half, z)
            for block in range(8):
                ma_ref[block, pl.ds(pl.multiple_of(y * 8, 8), 8), :] = packed[block]
            return carry

        lax.fori_loop(0, 4, per_y, 0)

    even = even_here()
    if on_even:
        pl.when(even)(lambda: slab(1))
    else:
        pl.when(jnp.logical_not(even))(lambda: slab(0))


def odd_inner_kernel(f_ref, g_ref, *refs):
    inner_kernel(f_ref, g_ref, refs[:-2], *refs[-2:], False)


def even_inner_kernel(_l, _ma, f_ref, g_ref, *refs):
    inner_kernel(f_ref, g_ref, refs[:-2], *refs[-2:], True)


def sweep_cells(l_ref, store):
    zs = zspeed()
    zcoef = shares(zs)
    zforward = zs > 0.0
    for block in range(8):
        ycoef = shares(yspeed(block))
        for half in range(2):
            cells = [[l_ref[half * 8 + block, pl.ds((4 * y + z) * 8, 8), :] for z in range(4)] for y in range(4)]
            done = sweep_yz(cells, ycoef, zcoef, zforward, block >= 4)
            for y in range(4):
                for z in range(4):
                    store(4 * y + z, half, block, done[y][z])


def sweep_kernel(l_ref, w_ref, g_ref, m_ref):
    def store(yz, half, block, value):
        g_ref[half * 8 + block, pl.ds(yz * 8, 8), :] = value

    sweep_cells(l_ref, store)
    m_ref[...] = weighed(w_ref, wide(g_ref, slice(None)))


def last_sweep_kernel(l_ref, o_ref, g_ref):
    def store(yz, half, block, value):
        g_ref[half * 8 + block, pl.ds(yz * 8, 8), :] = value

    sweep_cells(l_ref, store)
    for yz in range(NYZ):
        for group in range(2):
            rows = [g_ref[k % 2 * 8 + group * 4 + k // 2, pl.ds(yz * 8, 8), :] for k in range(8)]
            o_ref[:, pl.ds(yz * 16 + group * 8, 8), :] = jnp.swapaxes(jnp.stack(rows), 0, 1)


def sweep_edges(ra_ref, rb_ref, x_refs):
    even = jnp.full(TILE, (lax.axis_index("space") + 1) % 2, jnp.int32) > 0
    zs = zspeed()
    za, zb, zc = shares(zs)
    zforward = zs > 0.0
    for block in range(8):
        ya, yb, yc = shares(yspeed(block))
        step = -1 if block >= 4 else 1
        for half in range(2):
            cells = []
            for y in range(4):
                a, b = [r[block, pl.ds(y * 8, 8), :] for r in (ra_ref, rb_ref)]
                cells.append(jnp.where(even, b, a) if half else jnp.where(even, a, b))
            for y in range(4):
                mid = ya * cells[y] + yb * cells[(y + step) % 4] + yc * cells[(y + 2) % 4]
                near = jnp.where(zforward, pltpu.roll(mid, 2, 0), pltpu.roll(mid, 6, 0))
                x_refs[half][block, pl.ds(y * 8, 8), :] = za * mid + zb * near + zc * pltpu.roll(mid, 4, 0)


def unpacked(x_refs, y, z, half, block):
    shift = (-2 * z if half else 6 - 2 * z) % 8
    part = x_refs[half][block, pl.ds(pl.multiple_of(y * 8, 8), 8), :]
    part = pltpu.roll(part, shift, 0) if shift else part
    return jnp.where(xmask(half, 1), part, jnp.zeros(TILE, jnp.float32))


def edge_kernel(half, mi_ref, r_ref, w_ref, x_ref, m_ref):
    zs = zspeed()
    za, zb, zc = shares(zs)
    zforward = zs > 0.0
    for block in range(8):
        ya, yb, yc = shares(yspeed(block))
        step = -1 if block >= 4 else 1
        cells = [r_ref[block, pl.ds(y * 8, 8), :] for y in range(4)]
        for y in range(4):
            mid = ya * cells[y] + yb * cells[(y + step) % 4] + yc * cells[(y + 2) % 4]
            near = jnp.where(zforward, pltpu.roll(mid, 2, 0), pltpu.roll(mid, 6, 0))
            x_ref[block, pl.ds(y * 8, 8), :] = za * mid + zb * near + zc * pltpu.roll(mid, 4, 0)
    at = pl.ds(pl.multiple_of(half * 1024, 1024), 1024)
    sums = weighed(w_ref.at[:, at], wide(x_ref, slice(None)))
    source = lax.broadcasted_iota(jnp.int32, (32, CELLS), 0)
    cell = lax.broadcasted_iota(jnp.int32, (32, CELLS), 1)
    spread = (source // 2 * 8 + source % 2 + 6 * (1 - half) == cell).astype(jnp.bfloat16)
    thirds = jnp.dot(jnp.concatenate(split(sums)), spread, preferred_element_type=jnp.float32)
    total = mi_ref[...] + ((thirds[32:48, :] + thirds[16:32, :]) + thirds[0:16, :])
    m_ref[...] = total if len(m_ref.shape) == 2 else jnp.broadcast_to(total[None], m_ref.shape)


def chip_edge_kernel(*refs):
    edge_kernel(lax.axis_index("space") % 2, *refs)


def far_edge_kernel(*refs):
    edge_kernel(1 - lax.axis_index("space") % 2, *refs)


def last_kernel(s_ref, ra_ref, rb_ref, o_hbm, x0_ref, x1_ref, e_ref, sems):
    inside = pltpu.make_async_copy(s_ref.at[pl.ds(2, 4)], o_hbm.at[pl.ds(2, 4)], sems.at[4])
    inside.start()
    x_refs = (x0_ref, x1_ref)
    sweep_edges(ra_ref, rb_ref, x_refs)
    copies = []
    for half in (1, 0):
        for layer in range(2):
            at = layer if half else 2 + layer
            outer = layer if half else 6 + layer
            e_ref[at] = s_ref[outer]
            for y in range(4):
                for block in range(8):
                    rows = pl.ds(y * 64 + block * 2 + half, 4, stride=16)
                    part = x_refs[half][block, pl.ds(y * 8 + layer, 4, stride=2), :]
                    e_ref[at, rows, :] = e_ref[at, rows, :] + part
            copies.append(pltpu.make_async_copy(e_ref.at[at], o_hbm.at[outer], sems.at[at]))
            copies[-1].start()
    for copy in [inside] + copies:
        copy.wait()


F32, BF16 = jnp.float32, jnp.bfloat16
HBM = pl.BlockSpec(memory_space=pltpu.HBM)
GRID, MESSAGE, STORED = (16, CELLS, 128), (8, 32, 128), (LAYERS, 256, 128)
EVERYWHERE = (16, 16, CELLS)
EDGES = [pltpu.VMEM(MESSAGE, F32), pltpu.VMEM(MESSAGE, F32)]


def call(kernel, outs, scratch=(), hbm_in=False, hbm_out=False, **kw):
    if hbm_out:
        shapes = [jax.ShapeDtypeStruct(s, t) for s, t in outs]
    else:
        shapes = [pltpu.VMEM(s, t) for s, t in outs]

    def run(*args):
        space = pltpu.HBM if hbm_in else pltpu.VMEM
        args = [pltpu.with_memory_space_constraint(a, space) for a in args]
        return pl.pallas_call(
            kernel,
            out_shape=shapes,
            in_specs=[HBM if hbm_in else VMEM] * len(args),
            out_specs=[HBM if hbm_out else VMEM] * len(outs),
            scratch_shapes=list(scratch),
            compiler_params=pltpu.CompilerParams(vmem_limit_bytes=8 << 20),
            **kw,
        )(*args)

    return run


def local(distribution):
    layers, breadth, height, halves, _ = distribution.shape
    space_count = lax.axis_size("space")
    stored = distribution.reshape(layers, breadth, height, halves, 8, 128).transpose(0, 1, 2, 4, 3, 5)
    pairs_a = [(i, i ^ 1) for i in range(space_count)]
    pairs_b = [(i, i + 1) for i in range(1, space_count - 1, 2)]
    pairs_b = pairs_b + [(j, i) for i, j in pairs_b]
    g, weights, partial_moments = call(
        first_kernel,
        [(GRID, F32), ((48, 2048), BF16), (EVERYWHERE, F32)],
        [pltpu.VMEM(STORED, F32), pltpu.SemaphoreType.DMA((8,))],
        hbm_in=True,
    )(stored.reshape(STORED))
    sides = ()
    for step in range(STEPS):
        gathered = lax.all_to_all(partial_moments, "vel", 0, 0)
        fields, msg_b = call(outer_kernel, [((128, 128), F32), (MESSAGE, F32)])(gathered, g)
        inner_outs = [(GRID, F32), (MESSAGE, F32)]
        begun = call(odd_inner_kernel, inner_outs)(fields, g, *sides)
        got_b = lax.ppermute(msg_b, "space", pairs_b)
        moved, msg_a = call(even_inner_kernel, inner_outs, input_output_aliases={0: 0, 1: 1})(*begun, fields, g, *sides)
        got_a = lax.ppermute(msg_a, "space", pairs_a)
        if step + 1 < STEPS:
            g, inside = call(sweep_kernel, [(GRID, F32), ((16, CELLS), F32)])(
                moved, weights
            )
            outs = [(MESSAGE, F32), ((16, CELLS), F32)]
            near, inside = call(chip_edge_kernel, outs)(inside, got_a, weights)
            distant, partial_moments = call(far_edge_kernel, [(MESSAGE, F32), (EVERYWHERE, F32)])(
                inside, got_b, weights
            )
            sides = (near, distant)
        else:
            (swept,) = call(last_sweep_kernel, [(STORED, F32)], [pltpu.VMEM(GRID, F32)])(moved)
            (out,) = call(
                last_kernel,
                [(STORED, F32)],
                EDGES + [pltpu.VMEM((4, 256, 128), F32), pltpu.SemaphoreType.DMA((5,))],
                hbm_out=True,
            )(swept, got_a, got_b)
    out = out.reshape(layers, breadth, height, 8, halves, 128).transpose(0, 1, 2, 4, 3, 5)
    return out.reshape(distribution.shape)


def solution(mesh):
    return jax.shard_map(
        local,
        mesh=mesh,
        in_specs=(P("space", None, None, None, "vel"),),
        out_specs=P("space", None, None, None, "vel"),
        check_vma=False,
    )
```

```python
import math

import jax
import jax.numpy as jnp
from jax import lax
from jax.experimental import pallas as pl
from jax.experimental.pallas import tpu as pltpu
from jax.sharding import PartitionSpec as P


NV = 32
STEPS = 3
SPEED_LIMIT = 8.0
SPACING = 2.0 * SPEED_LIMIT / NV
LAM = 1.9 / ((NV - 1) * SPEED_LIMIT / NV)
QUAD = SPACING**3 / (2.0 * math.pi) ** 1.5
LOG2E = math.log2(math.e)
LAYERS, NYZ, CELLS = 8, 16, 128
VMEM = pl.BlockSpec(memory_space=pltpu.VMEM)
TILE = (8, 128)


def iota(axis):
    return lax.broadcasted_iota(jnp.int32, TILE, axis)


def shares(speed):
    n = LAM * jnp.abs(speed)
    return (1.0 - n) * (1.0 - 0.5 * n), n * (2.0 - n), 0.5 * n * (n - 1.0)


def yspeed(block):
    return -SPEED_LIMIT + ((4 * block + iota(1) // 32).astype(jnp.float32) + 0.5) * SPACING


def zspeed():
    return -SPEED_LIMIT + ((iota(1) % 32).astype(jnp.float32) + 0.5) * SPACING


def sweep_yz(cells, ycoef, zcoef, zforward, yforward):
    step = -1 if yforward else 1
    ya, yb, yc = ycoef
    za, zb, zc = zcoef
    mid = [
        [
            ya * cells[y][z] + yb * cells[(y + step) % 4][z] + yc * cells[(y + 2) % 4][z]
            for z in range(4)
        ]
        for y in range(4)
    ]
    return [
        [
            za * mid[y][z]
            + zb * jnp.where(zforward, mid[y][(z - 1) % 4], mid[y][(z + 1) % 4])
            + zc * mid[y][(z + 2) % 4]
            for z in range(4)
        ]
        for y in range(4)
    ]


def split(x):
    high = x.astype(jnp.bfloat16)
    rest = x - high.astype(jnp.float32)
    mid = rest.astype(jnp.bfloat16)
    return high, mid, (rest - mid.astype(jnp.float32)).astype(jnp.bfloat16)


def wide(ref, rows):
    return jnp.concatenate([ref[k, rows, :] for k in range(ref.shape[0])], axis=1)


def weighed(w_ref, x):
    n = w_ref.shape[0] // 3
    total = None
    for k, part in enumerate(split(x)):
        product = lax.dot_general(
            w_ref[0 : (3 - k) * n, :], part, (((1,), (1,)), ((), ())), preferred_element_type=jnp.float32
        )
        for j in range(3 - k):
            piece = product[j * n : (j + 1) * n, :]
            total = piece if total is None else total + piece
    return total


def xabs_here():
    index = jnp.full(TILE, lax.axis_index("vel"), jnp.int32)
    return (index.astype(jnp.float32) + 0.5) * SPACING


def even_here():
    return lax.axis_index("space") % 2 == 0


def first_kernel(d_hbm, g_ref, w_ref, m_ref, d_ref, sems):
    copies = []
    for k in range(8):
        part = (slice(None), pl.ds(k * 32, 32), slice(None))
        copies.append(pltpu.make_async_copy(d_hbm.at[part], d_ref.at[part], sems.at[k]))
    for copy in copies:
        copy.start()
    xabs = xabs_here()
    zs = zspeed()
    row = iota(0)
    for half in range(2):
        xs = xabs if half else -xabs
        for block in range(8):
            ys = yspeed(block)
            square = xs * xs + ys * ys + zs * zs
            low = [jnp.ones_like(xs), xs, ys, zs, xs * xs, ys * ys, zs * zs, xs * ys]
            high = [xs * zs, ys * zs, xs * square, ys * square, zs * square]
            tiles = []
            for rows in (low, high):
                tile = jnp.zeros(TILE, jnp.float32)
                for i, r in enumerate(rows):
                    tile = jnp.where(row == i, r, tile)
                tiles.append(QUAD * tile)
            for k, part in enumerate(split(jnp.concatenate(tiles))):
                w_ref[pl.ds(k * 16, 16), pl.ds(half * 1024 + block * 128, 128)] = part
    for k in range(8):
        copies[k].wait()
        for yz in (2 * k, 2 * k + 1):
            for group in range(2):
                turned = jnp.swapaxes(d_ref[:, pl.ds(yz * 16 + group * 8, 8), :], 0, 1)
                for k in range(8):
                    block, half = group * 4 + k // 2, k % 2
                    g_ref[half * 8 + block, pl.ds(yz * 8, 8), :] = turned[k]
    m_ref[...] = jnp.broadcast_to(weighed(w_ref, wide(g_ref, slice(None)))[None], m_ref.shape)


def cell_fields(m):
    rho = m[0]
    inv_rho = 1.0 / rho
    ux, uy, uz = m[1] * inv_rho, m[2] * inv_rho, m[3] * inv_rho
    energy = m[4] + m[5] + m[6]
    norm = ux * ux + uy * uy + uz * uz
    temp = (energy * inv_rho - norm) * (1.0 / 3.0)
    along = ux * m[1] + uy * m[2] + uz * m[3]

    def heating(third, u, first, r0, r1, r2):
        return 0.5 * (
            third
            - 2.0 * (ux * r0 + uy * r1 + uz * r2)
            - u * energy
            + norm * first
            + 2.0 * u * along
            - u * norm * rho
        )

    xq = heating(m[10], ux, m[1], m[4], m[7], m[8])
    yq = heating(m[11], uy, m[2], m[7], m[5], m[9])
    zq = heating(m[12], uz, m[3], m[8], m[9], m[6])
    root = jnp.sqrt(temp)
    inv_temp = 1.0 / temp
    conduction = (1.0 / 15.0) * (inv_rho * inv_temp) * inv_temp
    amp = (rho * inv_temp) * (root * inv_temp)
    retain = jnp.exp(-0.7 * rho * jnp.sqrt(root))
    k = -0.5 * LOG2E
    fold = conduction / k
    return [ux, uy, uz, k * inv_temp, fold * xq, fold * yq, fold * zq, amp * (1.0 - retain), retain]


class Cell:
    def __init__(self, tile, xabs, zs):
        (self.ux, self.uy, uz, self.scale, self.qx, self.qy, qz, self.amp, self.retain) = [
            jnp.broadcast_to(tile[:, k : k + 1], TILE) for k in range(9)
        ]
        zd = zs - uz
        self.ez, self.hz = zd * zd * self.scale, zd * qz
        self.x = []
        for xs in (-xabs, xabs):
            xd = xs - self.ux
            self.x.append((xd * xd * self.scale, xd * self.qx))

    def yz(self, block):
        yd = yspeed(block) - self.uy
        return yd * yd * self.scale + self.ez, yd * self.qy + self.hz

    def relax(self, half, yz, current):
        e = self.x[half][0] + yz[0]
        h = self.x[half][1] + yz[1]
        return self.amp * (jnp.exp2(e) * (1.0 + h * (e + 2.5 * LOG2E))) + self.retain * current


def xmask(half, far):
    row = iota(0)
    return (row < 1 + far) if half else (row > 6 - far)


def rotated(relaxed, half):
    return pltpu.roll(relaxed, 1 if half else 7, 0), pltpu.roll(relaxed, 2 if half else 6, 0)


def placed(out, half, z):
    shift = (2 * z if half else 2 * z + 2) % 8
    return pltpu.roll(out, shift, 0) if shift else out


def outer_kernel(a_ref, g_ref, f_ref, mb_ref):
    total = a_ref[0]
    for peer in range(1, a_ref.shape[0]):
        total = total + a_ref[peer]
    fields = cell_fields([total[k : k + 1, :] for k in range(13)])
    for k, value in enumerate(fields):
        f_ref[k : k + 1, :] = value
    f_ref[...] = jnp.transpose(f_ref[...])
    xabs = xabs_here()
    _, near, far = shares(xabs)
    zs = zspeed()

    def message(half):
        lower = 6 if half else 0
        near_rows = jnp.where((iota(0) < 4) if half else (iota(0) > 3), near, jnp.zeros(TILE, jnp.float32))

        def gathered(ref, y):
            return jnp.concatenate([ref[pl.ds(y * 32 + lower + layer, 4, stride=8), :] for layer in range(2)])

        for y in range(4):
            cell = Cell(gathered(f_ref, y), xabs, zs)
            for block in range(8):
                current = gathered(g_ref.at[half * 8 + block], y)
                relaxed = cell.relax(half, cell.yz(block), current)
                out = far * relaxed + near_rows * pltpu.roll(relaxed, 4, 0)
                for layer in range(2):
                    mb_ref[block, pl.ds(y * 8 + layer, 4, stride=2), :] = out[
                        layer * 4 : layer * 4 + 4, :
                    ]

    even = even_here()
    pl.when(even)(lambda: message(0))
    pl.when(jnp.logical_not(even))(lambda: message(1))


def inner_kernel(f_ref, g_ref, *refs):
    sides, (l_ref, ma_ref) = refs[:-2], refs[-2:]
    xabs = xabs_here()
    own, near, far = shares(xabs)
    zero = jnp.zeros(TILE, jnp.float32)
    zs = zspeed()
    inside = [
        (jnp.where(xmask(half, 0), zero, near), jnp.where(xmask(half, 1), zero, far)) for half in range(2)
    ]

    def slab(sent):
        x_refs = sides if sent else sides[::-1]
        n_out = jnp.where(xmask(sent, 0), near, zero)
        f_out = jnp.where(xmask(sent, 1), far, zero)

        def per_y(y, carry):
            packed = [zero] * 8
            for z in range(4):
                rows = pl.ds(pl.multiple_of(y * 32 + z * 8, 8), 8)
                cell = Cell(f_ref[rows, :], xabs, zs)
                for block in range(8):
                    yz = cell.yz(block)
                    for half in range(2):
                        at = half * 8 + block
                        current = g_ref[at, rows, :]
                        if x_refs:
                            current = current + unpacked(x_refs, y, z, half, block)
                        relaxed = cell.relax(half, yz, current)
                        r1, r2 = rotated(relaxed, half)
                        n_in, f_in = inside[half]
                        l_ref[at, rows, :] = own * relaxed + n_in * r1 + f_in * r2
                        if half == sent:
                            packed[block] = packed[block] + placed(n_out * r1 + f_out * r2, half, z)
            for block in range(8):
                ma_ref[block, pl.ds(pl.multiple_of(y * 8, 8), 8), :] = packed[block]
            return carry

        lax.fori_loop(0, 4, per_y, 0)

    even = even_here()
    pl.when(even)(lambda: slab(1))
    pl.when(jnp.logical_not(even))(lambda: slab(0))


def sweep_cells(l_ref, store):
    zs = zspeed()
    zcoef = shares(zs)
    zforward = zs > 0.0
    for block in range(8):
        ycoef = shares(yspeed(block))
        for half in range(2):
            cells = [[l_ref[half * 8 + block, pl.ds((4 * y + z) * 8, 8), :] for z in range(4)] for y in range(4)]
            done = sweep_yz(cells, ycoef, zcoef, zforward, block >= 4)
            for y in range(4):
                for z in range(4):
                    store(4 * y + z, half, block, done[y][z])


def sweep_kernel(l_ref, w_ref, g_ref, m_ref):
    def store(yz, half, block, value):
        g_ref[half * 8 + block, pl.ds(yz * 8, 8), :] = value

    sweep_cells(l_ref, store)
    m_ref[...] = weighed(w_ref, wide(g_ref, slice(None)))


def last_sweep_kernel(l_ref, o_ref, g_ref):
    def store(yz, half, block, value):
        g_ref[half * 8 + block, pl.ds(yz * 8, 8), :] = value

    sweep_cells(l_ref, store)
    for yz in range(NYZ):
        for group in range(2):
            rows = [g_ref[k % 2 * 8 + group * 4 + k // 2, pl.ds(yz * 8, 8), :] for k in range(8)]
            o_ref[:, pl.ds(yz * 16 + group * 8, 8), :] = jnp.swapaxes(jnp.stack(rows), 0, 1)


def sweep_edges(ra_ref, rb_ref, x_refs):
    even = jnp.full(TILE, (lax.axis_index("space") + 1) % 2, jnp.int32) > 0
    zs = zspeed()
    za, zb, zc = shares(zs)
    zforward = zs > 0.0
    for block in range(8):
        ya, yb, yc = shares(yspeed(block))
        step = -1 if block >= 4 else 1
        for half in range(2):
            cells = []
            for y in range(4):
                a, b = [r[block, pl.ds(y * 8, 8), :] for r in (ra_ref, rb_ref)]
                cells.append(jnp.where(even, b, a) if half else jnp.where(even, a, b))
            for y in range(4):
                mid = ya * cells[y] + yb * cells[(y + step) % 4] + yc * cells[(y + 2) % 4]
                near = jnp.where(zforward, pltpu.roll(mid, 2, 0), pltpu.roll(mid, 6, 0))
                x_refs[half][block, pl.ds(y * 8, 8), :] = za * mid + zb * near + zc * pltpu.roll(mid, 4, 0)


def unpacked(x_refs, y, z, half, block):
    shift = (-2 * z if half else 6 - 2 * z) % 8
    part = x_refs[half][block, pl.ds(pl.multiple_of(y * 8, 8), 8), :]
    part = pltpu.roll(part, shift, 0) if shift else part
    return jnp.where(xmask(half, 1), part, jnp.zeros(TILE, jnp.float32))


def edge_kernel(half, mi_ref, r_ref, w_ref, x_ref, m_ref):
    zs = zspeed()
    za, zb, zc = shares(zs)
    zforward = zs > 0.0
    for block in range(8):
        ya, yb, yc = shares(yspeed(block))
        step = -1 if block >= 4 else 1
        cells = [r_ref[block, pl.ds(y * 8, 8), :] for y in range(4)]
        for y in range(4):
            mid = ya * cells[y] + yb * cells[(y + step) % 4] + yc * cells[(y + 2) % 4]
            near = jnp.where(zforward, pltpu.roll(mid, 2, 0), pltpu.roll(mid, 6, 0))
            x_ref[block, pl.ds(y * 8, 8), :] = za * mid + zb * near + zc * pltpu.roll(mid, 4, 0)
    at = pl.ds(pl.multiple_of(half * 1024, 1024), 1024)
    sums = weighed(w_ref.at[:, at], wide(x_ref, slice(None)))
    source = lax.broadcasted_iota(jnp.int32, (32, CELLS), 0)
    cell = lax.broadcasted_iota(jnp.int32, (32, CELLS), 1)
    spread = (source // 2 * 8 + source % 2 + 6 * (1 - half) == cell).astype(jnp.bfloat16)
    thirds = jnp.dot(jnp.concatenate(split(sums)), spread, preferred_element_type=jnp.float32)
    total = mi_ref[...] + ((thirds[32:48, :] + thirds[16:32, :]) + thirds[0:16, :])
    m_ref[...] = total if len(m_ref.shape) == 2 else jnp.broadcast_to(total[None], m_ref.shape)


def chip_edge_kernel(*refs):
    edge_kernel(lax.axis_index("space") % 2, *refs)


def far_edge_kernel(*refs):
    edge_kernel(1 - lax.axis_index("space") % 2, *refs)


def last_kernel(s_ref, ra_ref, rb_ref, o_hbm, x0_ref, x1_ref, e_ref, sems):
    inside = pltpu.make_async_copy(s_ref.at[pl.ds(2, 4)], o_hbm.at[pl.ds(2, 4)], sems.at[4])
    inside.start()
    x_refs = (x0_ref, x1_ref)
    sweep_edges(ra_ref, rb_ref, x_refs)
    copies = []
    for half in (1, 0):
        for layer in range(2):
            at = layer if half else 2 + layer
            outer = layer if half else 6 + layer
            e_ref[at] = s_ref[outer]
            for y in range(4):
                for block in range(8):
                    rows = pl.ds(y * 64 + block * 2 + half, 4, stride=16)
                    part = x_refs[half][block, pl.ds(y * 8 + layer, 4, stride=2), :]
                    e_ref[at, rows, :] = e_ref[at, rows, :] + part
            copies.append(pltpu.make_async_copy(e_ref.at[at], o_hbm.at[outer], sems.at[at]))
            copies[-1].start()
    for copy in [inside] + copies:
        copy.wait()


F32, BF16 = jnp.float32, jnp.bfloat16
HBM = pl.BlockSpec(memory_space=pltpu.HBM)
GRID, MESSAGE, STORED = (16, CELLS, 128), (8, 32, 128), (LAYERS, 256, 128)
EVERYWHERE = (16, 16, CELLS)
EDGES = [pltpu.VMEM(MESSAGE, F32), pltpu.VMEM(MESSAGE, F32)]


def call(kernel, outs, scratch=(), hbm_in=False, hbm_out=False, **kw):
    if hbm_out:
        shapes = [jax.ShapeDtypeStruct(s, t) for s, t in outs]
    else:
        shapes = [pltpu.VMEM(s, t) for s, t in outs]

    def run(*args):
        space = pltpu.HBM if hbm_in else pltpu.VMEM
        args = [pltpu.with_memory_space_constraint(a, space) for a in args]
        return pl.pallas_call(
            kernel,
            out_shape=shapes,
            in_specs=[HBM if hbm_in else VMEM] * len(args),
            out_specs=[HBM if hbm_out else VMEM] * len(outs),
            scratch_shapes=list(scratch),
            compiler_params=pltpu.CompilerParams(vmem_limit_bytes=8 << 20),
            **kw,
        )(*args)

    return run


def local(distribution):
    layers, breadth, height, halves, _ = distribution.shape
    space_count = lax.axis_size("space")
    stored = distribution.reshape(layers, breadth, height, halves, 8, 128).transpose(0, 1, 2, 4, 3, 5)
    pairs_a = [(i, i ^ 1) for i in range(space_count)]
    pairs_b = [(i, i + 1) for i in range(1, space_count - 1, 2)]
    pairs_b = pairs_b + [(j, i) for i, j in pairs_b]
    g, weights, partial_moments = call(
        first_kernel,
        [(GRID, F32), ((48, 2048), BF16), (EVERYWHERE, F32)],
        [pltpu.VMEM(STORED, F32), pltpu.SemaphoreType.DMA((8,))],
        hbm_in=True,
    )(stored.reshape(STORED))
    sides = ()
    for step in range(STEPS):
        gathered = lax.all_to_all(partial_moments, "vel", 0, 0)
        fields, msg_b = call(outer_kernel, [((128, 128), F32), (MESSAGE, F32)])(gathered, g)
        got_b = lax.ppermute(msg_b, "space", pairs_b)
        moved, msg_a = call(inner_kernel, [(GRID, F32), (MESSAGE, F32)])(fields, g, *sides)
        got_a = lax.ppermute(msg_a, "space", pairs_a)
        if step + 1 < STEPS:
            g, inside = call(sweep_kernel, [(GRID, F32), ((16, CELLS), F32)])(
                moved, weights
            )
            outs = [(MESSAGE, F32), ((16, CELLS), F32)]
            near, inside = call(chip_edge_kernel, outs)(inside, got_a, weights)
            distant, partial_moments = call(far_edge_kernel, [(MESSAGE, F32), (EVERYWHERE, F32)])(
                inside, got_b, weights
            )
            sides = (near, distant)
        else:
            (swept,) = call(last_sweep_kernel, [(STORED, F32)], [pltpu.VMEM(GRID, F32)])(moved)
            (out,) = call(
                last_kernel,
                [(STORED, F32)],
                EDGES + [pltpu.VMEM((4, 256, 128), F32), pltpu.SemaphoreType.DMA((5,))],
                hbm_out=True,
            )(swept, got_a, got_b)
    out = out.reshape(layers, breadth, height, 8, halves, 128).transpose(0, 1, 2, 4, 3, 5)
    return out.reshape(distribution.shape)


def solution(mesh):
    return jax.shard_map(
        local,
        mesh=mesh,
        in_specs=(P("space", None, None, None, "vel"),),
        out_specs=P("space", None, None, None, "vel"),
        check_vma=False,
    )
```

```python
import math

import jax
import jax.numpy as jnp
from jax import lax
from jax.experimental import pallas as pl
from jax.experimental.pallas import tpu as pltpu
from jax.sharding import PartitionSpec as P


NV = 32
STEPS = 3
SPEED_LIMIT = 8.0
SPACING = 2.0 * SPEED_LIMIT / NV
LAM = 1.9 / ((NV - 1) * SPEED_LIMIT / NV)
QUAD = SPACING**3 / (2.0 * math.pi) ** 1.5
LOG2E = math.log2(math.e)
LAYERS, NYZ, CELLS = 8, 16, 128
VMEM = pl.BlockSpec(memory_space=pltpu.VMEM)
TILE = (8, 128)


def iota(axis):
    return lax.broadcasted_iota(jnp.int32, TILE, axis)


def shares(speed):
    n = LAM * jnp.abs(speed)
    return (1.0 - n) * (1.0 - 0.5 * n), n * (2.0 - n), 0.5 * n * (n - 1.0)


def yspeed(block):
    return -SPEED_LIMIT + ((4 * block + iota(1) // 32).astype(jnp.float32) + 0.5) * SPACING


def zspeed():
    return -SPEED_LIMIT + ((iota(1) % 32).astype(jnp.float32) + 0.5) * SPACING


def sweep_yz(cells, ycoef, zcoef, zforward, yforward):
    step = -1 if yforward else 1
    ya, yb, yc = ycoef
    za, zb, zc = zcoef
    mid = [
        [
            ya * cells[y][z] + yb * cells[(y + step) % 4][z] + yc * cells[(y + 2) % 4][z]
            for z in range(4)
        ]
        for y in range(4)
    ]
    return [
        [
            za * mid[y][z]
            + zb * jnp.where(zforward, mid[y][(z - 1) % 4], mid[y][(z + 1) % 4])
            + zc * mid[y][(z + 2) % 4]
            for z in range(4)
        ]
        for y in range(4)
    ]


def split(x):
    high = x.astype(jnp.bfloat16)
    rest = x - high.astype(jnp.float32)
    mid = rest.astype(jnp.bfloat16)
    return high, mid, (rest - mid.astype(jnp.float32)).astype(jnp.bfloat16)


def wide(ref, rows):
    return jnp.concatenate([ref[k, rows, :] for k in range(ref.shape[0])], axis=1)


def weighed(w_ref, x):
    n = w_ref.shape[0] // 3
    total = None
    for k, part in enumerate(split(x)):
        product = lax.dot_general(
            w_ref[0 : (3 - k) * n, :], part, (((1,), (1,)), ((), ())), preferred_element_type=jnp.float32
        )
        for j in range(3 - k):
            piece = product[j * n : (j + 1) * n, :]
            total = piece if total is None else total + piece
    return total


def in_a_row(m_ref, moments):
    for k in range(13):
        m_ref[:, k * CELLS : (k + 1) * CELLS] = moments[k : k + 1, :]


def xabs_here():
    index = jnp.full(TILE, lax.axis_index("vel"), jnp.int32)
    return (index.astype(jnp.float32) + 0.5) * SPACING


def even_here():
    return lax.axis_index("space") % 2 == 0


def first_kernel(d_hbm, g_ref, w_ref, m_ref, d_ref, sems):
    copies = []
    for k in range(8):
        part = (slice(None), pl.ds(k * 32, 32), slice(None))
        copies.append(pltpu.make_async_copy(d_hbm.at[part], d_ref.at[part], sems.at[k]))
    for copy in copies:
        copy.start()
    xabs = xabs_here()
    zs = zspeed()
    row = iota(0)
    for half in range(2):
        xs = xabs if half else -xabs
        for block in range(8):
            ys = yspeed(block)
            square = xs * xs + ys * ys + zs * zs
            low = [jnp.ones_like(xs), xs, ys, zs, xs * xs, ys * ys, zs * zs, xs * ys]
            high = [xs * zs, ys * zs, xs * square, ys * square, zs * square]
            tiles = []
            for rows in (low, high):
                tile = jnp.zeros(TILE, jnp.float32)
                for i, r in enumerate(rows):
                    tile = jnp.where(row == i, r, tile)
                tiles.append(QUAD * tile)
            for k, part in enumerate(split(jnp.concatenate(tiles))):
                w_ref[pl.ds(k * 16, 16), pl.ds(half * 1024 + block * 128, 128)] = part
    for k in range(8):
        copies[k].wait()
        for yz in (2 * k, 2 * k + 1):
            for group in range(2):
                turned = jnp.swapaxes(d_ref[:, pl.ds(yz * 16 + group * 8, 8), :], 0, 1)
                for k in range(8):
                    block, half = group * 4 + k // 2, k % 2
                    g_ref[half * 8 + block, pl.ds(yz * 8, 8), :] = turned[k]
    in_a_row(m_ref, weighed(w_ref, wide(g_ref, slice(None))))


def cell_fields(m):
    rho = m[0]
    inv_rho = 1.0 / rho
    ux, uy, uz = m[1] * inv_rho, m[2] * inv_rho, m[3] * inv_rho
    energy = m[4] + m[5] + m[6]
    norm = ux * ux + uy * uy + uz * uz
    temp = (energy * inv_rho - norm) * (1.0 / 3.0)
    along = ux * m[1] + uy * m[2] + uz * m[3]

    def heating(third, u, first, r0, r1, r2):
        return 0.5 * (
            third
            - 2.0 * (ux * r0 + uy * r1 + uz * r2)
            - u * energy
            + norm * first
            + 2.0 * u * along
            - u * norm * rho
        )

    xq = heating(m[10], ux, m[1], m[4], m[7], m[8])
    yq = heating(m[11], uy, m[2], m[7], m[5], m[9])
    zq = heating(m[12], uz, m[3], m[8], m[9], m[6])
    root = jnp.sqrt(temp)
    inv_temp = 1.0 / temp
    conduction = (1.0 / 15.0) * (inv_rho * inv_temp) * inv_temp
    amp = (rho * inv_temp) * (root * inv_temp)
    retain = jnp.exp(-0.7 * rho * jnp.sqrt(root))
    k = -0.5 * LOG2E
    fold = conduction / k
    return [ux, uy, uz, k * inv_temp, fold * xq, fold * yq, fold * zq, amp * (1.0 - retain), retain]


class Cell:
    def __init__(self, tile, xabs, zs):
        (self.ux, self.uy, uz, self.scale, self.qx, self.qy, qz, self.amp, self.retain) = [
            jnp.broadcast_to(tile[:, k : k + 1], TILE) for k in range(9)
        ]
        zd = zs - uz
        self.ez, self.hz = zd * zd * self.scale, zd * qz
        self.x = []
        for xs in (-xabs, xabs):
            xd = xs - self.ux
            self.x.append((xd * xd * self.scale, xd * self.qx))

    def yz(self, block):
        yd = yspeed(block) - self.uy
        return yd * yd * self.scale + self.ez, yd * self.qy + self.hz

    def relax(self, half, yz, current):
        e = self.x[half][0] + yz[0]
        h = self.x[half][1] + yz[1]
        return self.amp * (jnp.exp2(e) * (1.0 + h * (e + 2.5 * LOG2E))) + self.retain * current


def xmask(half, far):
    row = iota(0)
    return (row < 1 + far) if half else (row > 6 - far)


def rotated(relaxed, half):
    return pltpu.roll(relaxed, 1 if half else 7, 0), pltpu.roll(relaxed, 2 if half else 6, 0)


def placed(out, half, z):
    shift = (2 * z if half else 2 * z + 2) % 8
    return pltpu.roll(out, shift, 0) if shift else out


def outer_kernel(a_ref, g_ref, f_ref, mb_ref):
    total = a_ref[0]
    for peer in range(1, a_ref.shape[0]):
        total = total + a_ref[peer]
    fields = cell_fields([total[:, k * CELLS : (k + 1) * CELLS] for k in range(13)])
    for k, value in enumerate(fields):
        f_ref[k : k + 1, :] = value
    f_ref[...] = jnp.transpose(f_ref[...])
    xabs = xabs_here()
    _, near, far = shares(xabs)
    zs = zspeed()

    def message(half):
        lower = 6 if half else 0
        near_rows = jnp.where((iota(0) < 4) if half else (iota(0) > 3), near, jnp.zeros(TILE, jnp.float32))

        def gathered(ref, y):
            return jnp.concatenate([ref[pl.ds(y * 32 + lower + layer, 4, stride=8), :] for layer in range(2)])

        for y in range(4):
            cell = Cell(gathered(f_ref, y), xabs, zs)
            for block in range(8):
                current = gathered(g_ref.at[half * 8 + block], y)
                relaxed = cell.relax(half, cell.yz(block), current)
                out = far * relaxed + near_rows * pltpu.roll(relaxed, 4, 0)
                for layer in range(2):
                    mb_ref[block, pl.ds(y * 8 + layer, 4, stride=2), :] = out[
                        layer * 4 : layer * 4 + 4, :
                    ]

    even = even_here()
    pl.when(even)(lambda: message(0))
    pl.when(jnp.logical_not(even))(lambda: message(1))


def inner_kernel(f_ref, g_ref, *refs):
    sides, (l_ref, ma_ref) = refs[:-2], refs[-2:]
    xabs = xabs_here()
    own, near, far = shares(xabs)
    zero = jnp.zeros(TILE, jnp.float32)
    zs = zspeed()
    inside = [
        (jnp.where(xmask(half, 0), zero, near), jnp.where(xmask(half, 1), zero, far)) for half in range(2)
    ]

    def slab(sent):
        x_refs = sides if sent else sides[::-1]
        n_out = jnp.where(xmask(sent, 0), near, zero)
        f_out = jnp.where(xmask(sent, 1), far, zero)

        def per_y(y, carry):
            packed = [zero] * 8
            for z in range(4):
                rows = pl.ds(pl.multiple_of(y * 32 + z * 8, 8), 8)
                cell = Cell(f_ref[rows, :], xabs, zs)
                for block in range(8):
                    yz = cell.yz(block)
                    for half in range(2):
                        at = half * 8 + block
                        current = g_ref[at, rows, :]
                        if x_refs:
                            current = current + unpacked(x_refs, y, z, half, block)
                        relaxed = cell.relax(half, yz, current)
                        r1, r2 = rotated(relaxed, half)
                        n_in, f_in = inside[half]
                        l_ref[at, rows, :] = own * relaxed + n_in * r1 + f_in * r2
                        if half == sent:
                            packed[block] = packed[block] + placed(n_out * r1 + f_out * r2, half, z)
            for block in range(8):
                ma_ref[block, pl.ds(pl.multiple_of(y * 8, 8), 8), :] = packed[block]
            return carry

        lax.fori_loop(0, 4, per_y, 0)

    even = even_here()
    pl.when(even)(lambda: slab(1))
    pl.when(jnp.logical_not(even))(lambda: slab(0))


def sweep_cells(l_ref, store):
    zs = zspeed()
    zcoef = shares(zs)
    zforward = zs > 0.0
    for block in range(8):
        ycoef = shares(yspeed(block))
        for half in range(2):
            cells = [[l_ref[half * 8 + block, pl.ds((4 * y + z) * 8, 8), :] for z in range(4)] for y in range(4)]
            done = sweep_yz(cells, ycoef, zcoef, zforward, block >= 4)
            for y in range(4):
                for z in range(4):
                    store(4 * y + z, half, block, done[y][z])


def sweep_kernel(l_ref, w_ref, g_ref, m_ref):
    def store(yz, half, block, value):
        g_ref[half * 8 + block, pl.ds(yz * 8, 8), :] = value

    sweep_cells(l_ref, store)
    m_ref[...] = weighed(w_ref, wide(g_ref, slice(None)))


def last_sweep_kernel(l_ref, o_ref, g_ref):
    def store(yz, half, block, value):
        g_ref[half * 8 + block, pl.ds(yz * 8, 8), :] = value

    sweep_cells(l_ref, store)
    for yz in range(NYZ):
        for group in range(2):
            rows = [g_ref[k % 2 * 8 + group * 4 + k // 2, pl.ds(yz * 8, 8), :] for k in range(8)]
            o_ref[:, pl.ds(yz * 16 + group * 8, 8), :] = jnp.swapaxes(jnp.stack(rows), 0, 1)


def sweep_edges(ra_ref, rb_ref, x_refs):
    even = jnp.full(TILE, (lax.axis_index("space") + 1) % 2, jnp.int32) > 0
    zs = zspeed()
    za, zb, zc = shares(zs)
    zforward = zs > 0.0
    for block in range(8):
        ya, yb, yc = shares(yspeed(block))
        step = -1 if block >= 4 else 1
        for half in range(2):
            cells = []
            for y in range(4):
                a, b = [r[block, pl.ds(y * 8, 8), :] for r in (ra_ref, rb_ref)]
                cells.append(jnp.where(even, b, a) if half else jnp.where(even, a, b))
            for y in range(4):
                mid = ya * cells[y] + yb * cells[(y + step) % 4] + yc * cells[(y + 2) % 4]
                near = jnp.where(zforward, pltpu.roll(mid, 2, 0), pltpu.roll(mid, 6, 0))
                x_refs[half][block, pl.ds(y * 8, 8), :] = za * mid + zb * near + zc * pltpu.roll(mid, 4, 0)


def unpacked(x_refs, y, z, half, block):
    shift = (-2 * z if half else 6 - 2 * z) % 8
    part = x_refs[half][block, pl.ds(pl.multiple_of(y * 8, 8), 8), :]
    part = pltpu.roll(part, shift, 0) if shift else part
    return jnp.where(xmask(half, 1), part, jnp.zeros(TILE, jnp.float32))


def edge_kernel(half, mi_ref, r_ref, w_ref, x_ref, m_ref):
    zs = zspeed()
    za, zb, zc = shares(zs)
    zforward = zs > 0.0
    for block in range(8):
        ya, yb, yc = shares(yspeed(block))
        step = -1 if block >= 4 else 1
        cells = [r_ref[block, pl.ds(y * 8, 8), :] for y in range(4)]
        for y in range(4):
            mid = ya * cells[y] + yb * cells[(y + step) % 4] + yc * cells[(y + 2) % 4]
            near = jnp.where(zforward, pltpu.roll(mid, 2, 0), pltpu.roll(mid, 6, 0))
            x_ref[block, pl.ds(y * 8, 8), :] = za * mid + zb * near + zc * pltpu.roll(mid, 4, 0)
    at = pl.ds(pl.multiple_of(half * 1024, 1024), 1024)
    sums = weighed(w_ref.at[:, at], wide(x_ref, slice(None)))
    source = lax.broadcasted_iota(jnp.int32, (32, CELLS), 0)
    cell = lax.broadcasted_iota(jnp.int32, (32, CELLS), 1)
    spread = (source // 2 * 8 + source % 2 + 6 * (1 - half) == cell).astype(jnp.bfloat16)
    thirds = jnp.dot(jnp.concatenate(split(sums)), spread, preferred_element_type=jnp.float32)
    total = mi_ref[...] + ((thirds[32:48, :] + thirds[16:32, :]) + thirds[0:16, :])
    if m_ref.shape == total.shape:
        m_ref[...] = total
    else:
        in_a_row(m_ref, total)


def chip_edge_kernel(*refs):
    edge_kernel(lax.axis_index("space") % 2, *refs)


def far_edge_kernel(*refs):
    edge_kernel(1 - lax.axis_index("space") % 2, *refs)


def last_kernel(s_ref, ra_ref, rb_ref, o_hbm, x0_ref, x1_ref, e_ref, sems):
    inside = pltpu.make_async_copy(s_ref.at[pl.ds(2, 4)], o_hbm.at[pl.ds(2, 4)], sems.at[4])
    inside.start()
    x_refs = (x0_ref, x1_ref)
    sweep_edges(ra_ref, rb_ref, x_refs)
    copies = []
    for half in (1, 0):
        for layer in range(2):
            at = layer if half else 2 + layer
            outer = layer if half else 6 + layer
            e_ref[at] = s_ref[outer]
            for y in range(4):
                for block in range(8):
                    rows = pl.ds(y * 64 + block * 2 + half, 4, stride=16)
                    part = x_refs[half][block, pl.ds(y * 8 + layer, 4, stride=2), :]
                    e_ref[at, rows, :] = e_ref[at, rows, :] + part
            copies.append(pltpu.make_async_copy(e_ref.at[at], o_hbm.at[outer], sems.at[at]))
            copies[-1].start()
    for copy in [inside] + copies:
        copy.wait()


F32, BF16 = jnp.float32, jnp.bfloat16
HBM = pl.BlockSpec(memory_space=pltpu.HBM)
GRID, MESSAGE, STORED = (16, CELLS, 128), (8, 32, 128), (LAYERS, 256, 128)
ROW = (1, 13 * CELLS)
EDGES = [pltpu.VMEM(MESSAGE, F32), pltpu.VMEM(MESSAGE, F32)]


def call(kernel, outs, scratch=(), hbm_in=False, hbm_out=False, **kw):
    if hbm_out:
        shapes = [jax.ShapeDtypeStruct(s, t) for s, t in outs]
    else:
        shapes = [pltpu.VMEM(s, t) for s, t in outs]

    def run(*args):
        space = pltpu.HBM if hbm_in else pltpu.VMEM
        args = [pltpu.with_memory_space_constraint(a, space) for a in args]
        return pl.pallas_call(
            kernel,
            out_shape=shapes,
            in_specs=[HBM if hbm_in else VMEM] * len(args),
            out_specs=[HBM if hbm_out else VMEM] * len(outs),
            scratch_shapes=list(scratch),
            compiler_params=pltpu.CompilerParams(vmem_limit_bytes=8 << 20),
            **kw,
        )(*args)

    return run


def local(distribution):
    layers, breadth, height, halves, _ = distribution.shape
    space_count = lax.axis_size("space")
    stored = distribution.reshape(layers, breadth, height, halves, 8, 128).transpose(0, 1, 2, 4, 3, 5)
    pairs_a = [(i, i ^ 1) for i in range(space_count)]
    pairs_b = [(i, i + 1) for i in range(1, space_count - 1, 2)]
    pairs_b = pairs_b + [(j, i) for i, j in pairs_b]
    g, weights, partial_moments = call(
        first_kernel,
        [(GRID, F32), ((48, 2048), BF16), (ROW, F32)],
        [pltpu.VMEM(STORED, F32), pltpu.SemaphoreType.DMA((8,))],
        hbm_in=True,
    )(stored.reshape(STORED))
    sides = ()
    for step in range(STEPS):
        everywhere = jnp.broadcast_to(partial_moments[None], (lax.axis_size("vel"),) + ROW)
        gathered = lax.all_to_all(everywhere, "vel", 0, 0)
        fields, msg_b = call(outer_kernel, [((128, 128), F32), (MESSAGE, F32)])(gathered, g)
        got_b = lax.ppermute(msg_b, "space", pairs_b)
        moved, msg_a = call(inner_kernel, [(GRID, F32), (MESSAGE, F32)])(fields, g, *sides)
        got_a = lax.ppermute(msg_a, "space", pairs_a)
        if step + 1 < STEPS:
            g, inside = call(sweep_kernel, [(GRID, F32), ((16, CELLS), F32)])(
                moved, weights
            )
            outs = [(MESSAGE, F32), ((16, CELLS), F32)]
            near, inside = call(chip_edge_kernel, outs)(inside, got_a, weights)
            distant, partial_moments = call(far_edge_kernel, [(MESSAGE, F32), (ROW, F32)])(inside, got_b, weights)
            sides = (near, distant)
        else:
            (swept,) = call(last_sweep_kernel, [(STORED, F32)], [pltpu.VMEM(GRID, F32)])(moved)
            (out,) = call(
                last_kernel,
                [(STORED, F32)],
                EDGES + [pltpu.VMEM((4, 256, 128), F32), pltpu.SemaphoreType.DMA((5,))],
                hbm_out=True,
            )(swept, got_a, got_b)
    out = out.reshape(layers, breadth, height, 8, halves, 128).transpose(0, 1, 2, 4, 3, 5)
    return out.reshape(distribution.shape)


def solution(mesh):
    return jax.shard_map(
        local,
        mesh=mesh,
        in_specs=(P("space", None, None, None, "vel"),),
        out_specs=P("space", None, None, None, "vel"),
        check_vma=False,
    )
```
